512 devices in a mesh: wide: 64 (over x, y, core), narrow: 8 (over z).
Axes of the slice: x: 4, y: 8, z: 8, core: 2. Of those that a mesh axis runs over, the one named last changes fastest.
Arguments:
- orbitals: float32 [448, 56, 7, 512], P('wide', 'narrow'), may hold values from -6 to 6
- cell_matrix: bfloat16 [64, 8, 1, 512, 512], P('wide', 'narrow'), as said below
- cell_order: int32 [64, 8, 1, 512], P('wide', 'narrow'), may hold values from 0 to 511, as said below
Outputs:
- filtered_basis: float32 [448, 56, 7, 512], P('wide', 'narrow')
The draws below stay inside these ranges and needn't reach their ends.
Inputs may be any that keep to these rules, and one draw needn't show every extreme that they name: Each row of cell_order lists the 512 cell node numbers of one cell in the order given by one of the 48 rotations and reflections of the cube. `cell_matrix`: each cell's matrix is symmetric.
All inputs are finite; a program needn't handle non-finite values.
Results may differ from the reference program's by a relative error of at most 0.00045.
The reference program's roundings to bfloat16 on the way count: a program that leaves them out, or rounds other values in their place, can miss the bound.
Values sent between devices are 32-bit elements; how exact they have to be, the bound alone decides.
A program may use at most 64 MiB of HBM per device.

```python
import math
import jax
import jax.numpy as jnp
from jax import lax

ORDER = 7
PE = 8
CELLN = 512
NB = 512
C = 1
DEG = 4
ZN = 7
CELLS_X = 64
CELLS_Y = 8
GX = 448
GY = 56
NODES = 175616


def draw_cell_matrix(key, part):
    array_shape = (CELLS_X, CELLS_Y, C, CELLN, CELLN)
    key_one, key_two = jax.random.split(key)
    samples = jax.random.normal(key_one, array_shape, jnp.float32)
    diagonal = jax.random.uniform(key_two, array_shape[:-1], jnp.float32, 1.0, 2.0)
    symmetric = (samples + jnp.swapaxes(samples, -1, -2)) * (0.5 / math.sqrt(2.0 * CELLN))
    positions = jnp.arange(CELLN, dtype=jnp.int32)
    on_diagonal = positions[:, None] == positions[None, :]
    matrix_out = jnp.where(on_diagonal, diagonal[..., :, None], symmetric)
    return matrix_out.astype(jnp.bfloat16)


def draw_cell_order(key, part):
    cell_count = CELLS_X * CELLS_Y * C
    key_one, key_two = jax.random.split(key)
    axes_pick = jax.random.randint(key_one, (cell_count,), 0, 6)
    flip_bits = jax.random.randint(key_two, (cell_count, 3), 0, 2)
    symmetry_table = jnp.array([[0, 1, 2], [0, 2, 1], [1, 0, 2], [1, 2, 0], [2, 0, 1], [2, 1, 0]], dtype=jnp.int32)
    selected = symmetry_table[axes_pick]
    positions = jnp.arange(CELLN, dtype=jnp.int32)
    coordinates = jnp.stack([positions // (PE * PE), positions // PE % PE, positions % PE], axis=-1)
    spread = jnp.broadcast_to(coordinates[None], (cell_count, CELLN, 3))
    picked = jnp.take_along_axis(spread, jnp.broadcast_to(selected[:, None, :], (cell_count, CELLN, 3)), axis=2)
    flipped = jnp.where(flip_bits[:, None, :] == 1, PE - 1 - picked, picked)
    number = flipped[..., 0] * PE * PE + flipped[..., 1] * PE + flipped[..., 2]
    return number.reshape(CELLS_X, CELLS_Y, C, CELLN).astype(jnp.int32)


def block_scale(key, shape, cuts, least, high):
    def one(dim, shards_of):
        heights = jax.random.uniform(jax.random.fold_in(jax.random.fold_in(key, 6), dim), (shards_of,), jnp.float32, least / len(cuts), high / len(cuts))
        return jnp.repeat(jnp.exp(heights), shape[dim] // shards_of).reshape((-1,) + (1,) * (len(shape) - dim - 1))

    loudness = one(*cuts[0])
    for cut in cuts[1:]:
        loudness = loudness * one(*cut)
    return loudness


def noise(rng, shape, scale, bound, cuts=(), held_as=jnp.bfloat16):
    values = jax.random.normal(rng, shape, jnp.float32) * scale
    if len(cuts) > 0:
        values = block_scale(rng, shape, cuts, -0.22, 0.18) * values
    return jnp.clip(values, min=-bound, max=bound).astype(held_as)


def setup_inputs(seed: int = 0) -> dict:
    splits = jax.random.split(jax.random.key(seed), 4)
    orbitals = noise(splits[0], (GX, GY, ZN, NB), 1.0, 6.0, ((0, 64), (1, 8)), jnp.float32)
    cell_matrix = draw_cell_matrix(jax.random.fold_in(splits[3], 71), 0)
    cell_order = draw_cell_order(jax.random.fold_in(splits[3], 71), 0)
    return dict(orbitals=orbitals, cell_matrix=cell_matrix, cell_order=cell_order)


band_low = 4.0
band_high = 34.0
anchor = 0.0

def apply_cells(vector, matrices, cell_order, inverse_order):
    z_window = (ORDER * jnp.arange(C, dtype=jnp.int32)[:, None] + jnp.arange(PE, dtype=jnp.int32)[None, :]) % ZN
    y_window = (ORDER * jnp.arange(CELLS_Y, dtype=jnp.int32)[:, None] + jnp.arange(PE, dtype=jnp.int32)[None, :]) % GY

    def one_column(carry, column):
        x_window = (ORDER * column + jnp.arange(PE, dtype=jnp.int32)) % GX
        x_slab = jnp.take(vector, x_window, axis=0)
        cell_boxes = x_slab[:, y_window][:, :, :, z_window]
        cell_boxes = jnp.transpose(cell_boxes, (1, 3, 0, 2, 4, 5)).reshape(CELLS_Y, C, CELLN, NB)
        rounded = lax.optimization_barrier(cell_boxes.astype(jnp.bfloat16)).astype(jnp.float32)
        ordering = lax.dynamic_index_in_dim(cell_order, column, 0, keepdims=False)
        inverse_now = lax.dynamic_index_in_dim(inverse_order, column, 0, keepdims=False)
        matrices_f = lax.dynamic_index_in_dim(matrices, column, 0, keepdims=False).astype(jnp.float32)
        gathered = jnp.take_along_axis(rounded, ordering[..., None], axis=2)
        products = jnp.einsum('jckm,jcmn->jckn', matrices_f, gathered, precision=lax.Precision.HIGHEST)
        placed = jnp.take_along_axis(products, inverse_now[..., None], axis=2)
        placed = placed.reshape(CELLS_Y, C, PE, PE, PE, NB)
        placed = jnp.transpose(placed, (2, 0, 3, 1, 4, 5))
        carry = carry.at[x_window[:, None, None, None, None], y_window[None, :, :, None, None], z_window[None, None, None, :, :]].add(placed)
        return (carry, None)
    start = jnp.zeros(vector.shape, jnp.float32)
    result, _ = lax.scan(one_column, start, jnp.arange(CELLS_X, dtype=jnp.int32))
    return result

def reference(orbitals, cell_matrix, cell_order):
    inverse_order = jnp.argsort(cell_order, axis=-1).astype(jnp.int32)
    center = (band_low + band_high) / 2.0
    half_width = (band_high - band_low) / 2.0
    sigma_now = half_width / (anchor - center)
    tau_value = 2.0 / sigma_now

    def shifted_h(vector):
        return apply_cells(vector, cell_matrix, cell_order, inverse_order) - center * vector
    previous = orbitals
    current = shifted_h(previous) * (sigma_now / half_width)
    for degree_step in range(DEG - 1):
        sigma_new = 1.0 / (tau_value - sigma_now)
        updated = shifted_h(current) * (2.0 * sigma_new / half_width) - sigma_now * sigma_new * previous
        previous, current = (current, updated)
        sigma_now = sigma_new
    flattened = current.reshape(-1, NB)
    correlation = jnp.einsum('kn,km->nm', flattened, flattened, precision=lax.Precision.HIGHEST) / NODES
    lower_factor = jnp.linalg.cholesky(correlation)
    identity_matrix = jnp.eye(NB, dtype=jnp.float32)
    r_inverse = lax.linalg.triangular_solve(lower_factor, identity_matrix, left_side=True, lower=True).T
    result = jnp.dot(flattened, r_inverse, precision=lax.Precision.HIGHEST)
    return result.reshape(current.shape)
```

```python
import functools

import jax
import jax.numpy as jnp
from jax import lax
from jax.experimental import pallas as pl
from jax.experimental.pallas import tpu as pltpu
from jax.sharding import PartitionSpec as P

DEG = 4
MESH=pl.DeviceIdType.MESH
XS,YS,ZS=4,8,8
TILES=160
HALF=TILES//2
CA=HALF//XS
CB=3

def place():
    w=lax.axis_index("wide"); z=lax.axis_index("narrow")
    x=w//16; y=(w//2)%8; core=w%2
    return x,y,z,core

def at(x,y,z,core):
    return {"wide": x*16+y*2+core, "narrow": z}

def peers(x,y,z,core):
    out=[at(x,y,z,1-core)]
    for d in range(1,XS): out.append(at((x+d)%XS,y,z,core))
    for d in range(1,YS): out.append(at(x,(y+d)%YS,z,core))
    for d in range(1,ZS): out.append(at(x,y,(z+d)%ZS,core))
    return out

def ar_scratch():
    f=jnp.float32
    return [pltpu.VMEM((HALF,8,128),f),
            pltpu.VMEM((HALF,8,128),f),
            pltpu.VMEM((XS,CA,8,128),f),
            pltpu.VMEM((YS*CB,8,128),f),
            pltpu.VMEM((YS,CB,8,128),f),
            pltpu.VMEM((CB,8,128),f),
            pltpu.VMEM((ZS,CB,8,128),f),
            pltpu.VMEM((YS*CB,8,128),f),
            pltpu.SemaphoreType.DMA((40,)),
            pltpu.SemaphoreType.DMA((40,))]

def all_reduce(g, full, rc, acc, rx, sx, ry, sy, rz, gy, ssem, rsem):
    x,y,z,core=place()
    pend=[]
    cnt=[0]
    def send(src,dst,to):
        k=cnt[0]; cnt[0]+=1
        c=pltpu.make_async_remote_copy(src_ref=src,dst_ref=dst,send_sem=ssem.at[k],recv_sem=rsem.at[k],device_id=to,device_id_type=MESH)
        c.start(); pend.append(c)
        return c
    other=1-core
    c=send(g.at[pl.ds(other*HALF,HALF)],rc,at(x,y,z,other))
    c.wait_recv()
    acc[...]=g[pl.ds(core*HALF,HALF)]+rc[...]
    cs=[send(acc.at[pl.ds(((x+d)%XS)*CA,CA)],rx.at[d],at((x+d)%XS,y,z,core)) for d in range(1,XS)]
    for c in cs: c.wait_recv()
    s=acc[pl.ds(x*CA,CA)]
    for d in range(1,XS): s=s+rx[d]
    sx[0:CA]=s
    sx[CA:]=jnp.zeros((YS*CB-CA,8,128),jnp.float32)
    cs=[send(sx.at[pl.ds(((y+d)%YS)*CB,CB)],ry.at[d],at(x,(y+d)%YS,z,core)) for d in range(1,YS)]
    for c in cs: c.wait_recv()
    s=sx[pl.ds(y*CB,CB)]
    for d in range(1,YS): s=s+ry[d]
    sy[...]=s
    cs=[send(sy,rz.at[d],at(x,y,(z+d)%ZS,core)) for d in range(1,ZS)]
    for c in cs: c.wait_recv()
    for d in range(1,ZS): s=s+rz[d]
    gy[pl.ds(y*CB,CB)]=s
    cs=[send(gy.at[pl.ds(y*CB,CB)],gy.at[pl.ds(y*CB,CB)],at(x,(y+d)%YS,z,core)) for d in range(1,YS)]
    for c in cs: c.wait_recv()
    mine=core*HALF+x*CA
    full[pl.ds(mine,CA)]=gy[0:CA]
    cs=[send(gy.at[pl.ds(0,CA)],full.at[pl.ds(mine,CA)],at((x+d)%XS,y,z,core)) for d in range(1,XS)]
    f0=send(gy.at[pl.ds(0,CA)],full.at[pl.ds(mine,CA)],at(x,y,z,other))
    fs=[f0]
    for d in range(1,XS):
        cs[d-1].wait_recv()
        src=core*HALF+((x-d+XS)%XS)*CA
        fs.append(send(full.at[pl.ds(src,CA)],full.at[pl.ds(src,CA)],at(x,y,z,other)))
    for c in fs: c.wait_recv()
    for c in pend: c.wait_send()

def barrier(ps):
    sem=pltpu.get_barrier_semaphore()
    for p in ps: pl.semaphore_signal(sem,inc=1,device_id=p,device_id_type=MESH)
    pl.semaphore_wait(sem,len(ps))

def ar_kernel(g,full,*scr):
    barrier(peers(*place()))
    all_reduce(g,full,*scr)

def ar_call(g):
    return pl.pallas_call(ar_kernel,out_shape=jax.ShapeDtypeStruct((TILES,8,128),jnp.float32),
        in_specs=[pl.BlockSpec(memory_space=pltpu.VMEM)],out_specs=pl.BlockSpec(memory_space=pltpu.VMEM),
        scratch_shapes=ar_scratch(),
        compiler_params=pltpu.CompilerParams(collective_id=0,has_side_effects=True,vmem_limit_bytes=40<<20))(g)


def dot_nn(a, b):
    return lax.dot_general(
        a, b, (((1,), (0,)), ((), ())), precision=lax.Precision.HIGHEST, preferred_element_type=jnp.float32
    )


def dot_nt(a, b):
    return lax.dot_general(
        a, b, (((1,), (1,)), ((), ())), precision=lax.Precision.HIGHEST, preferred_element_type=jnp.float32
    )


def reciprocal(d):
    r = pl.reciprocal(d, approx=True)
    r = r * (2.0 - d * r)
    return r * (2.0 - d * r)


def inverse_factor(block):
    rows = [block[8 * i : 8 * i + 8, :] for i in range(16)]
    lane = lax.broadcasted_iota(jnp.int32, (8, 128), 1)
    sub = lax.broadcasted_iota(jnp.int32, (8, 128), 0)
    for b in range(16):
        first = 8 * b
        panel = [jnp.broadcast_to(rows[b][i : i + 1, :], (8, 128)) for i in range(8)]
        e = {}
        for i in range(8):
            for j in range(i, 8):
                e[i, j] = jnp.broadcast_to(panel[i][:, first + j : first + j + 1], (8, 128))
        inside = (lane >= first) & (lane < first + 8)
        p = [jnp.where(inside, jnp.where(lane == first + i, 1.0, 0.0), panel[i]) for i in range(8)]
        inv = [None] * 8
        m = {}
        for k in range(8):
            inv[k] = reciprocal(e[k, k])
            for i in range(k + 1, 8):
                m[i, k] = e[k, i] * inv[k]
                for j in range(i, 8):
                    e[i, j] = e[i, j] - m[i, k] * e[k, j]
                p[i] = p[i] - m[i, k] * p[k]
        if b < 15:
            s = [p[k] * inv[k] for k in range(8)]
            for l in range(6, -1, -1):
                for k in range(7, l, -1):
                    s[l] = s[l] - m[k, l] * s[k]
            for i in range(b + 1, 16):
                below = rows[i]
                total = jnp.where(inside, 0.0, below)
                for k in range(8):
                    total = total - jnp.broadcast_to(below[:, first + k : first + k + 1], (8, 128)) * s[k]
                rows[i] = total
        own, pivot = p[0], e[0, 0]
        for k in range(1, 8):
            own = jnp.where(sub == k, p[k], own)
            pivot = jnp.where(sub == k, e[k, k], pivot)
        y = lax.rsqrt(pivot)
        y = y * (1.5 - 0.5 * pivot * y * y)
        rows[b] = jnp.where(lane <= sub + first, own, 0.0) * y
    return jnp.concatenate(rows, axis=0)


def finish_kernel(node_total, packed, field, out, w, x, f):
    for i in range(4):
        for j in range(i + 1):
            at_tile = 16 * (i * (i + 1) // 2 + j)
            w[128 * i : 128 * i + 128, 128 * j : 128 * j + 128] = (
                packed[at_tile : at_tile + 16].reshape(128, 128) * (1.0 / node_total)
            )
    for i in range(7):
        for j in range(7):
            r = 8 * (7 * i + j)
            f[r : r + 7, :] = field[i, j]
            f[r + 7 : r + 8, :] = jnp.zeros((1, 512), jnp.float32)
    lower = {}
    for j in range(4):
        here = slice(128 * j, 128 * j + 128)
        inverse = inverse_factor(w[here, here])
        if j < 3:
            column = dot_nt(w[128 * (j + 1) :, here], inverse)
            lower[j] = column
            for i in range(j + 1, 4):
                band = column[128 * (i - j - 1) : 128 * (i - j)]
                w[128 * i : 128 * i + 128, 128 * (j + 1) : 128 * (i + 1)] = w[
                    128 * i : 128 * i + 128, 128 * (j + 1) : 128 * (i + 1)
                ] - dot_nt(band, column[: 128 * (i - j)])
        x[here, here] = inverse
        if j > 0:
            left = jnp.concatenate([lower[k][128 * (j - k - 1) : 128 * (j - k)] for k in range(j)], axis=1)
            x[here, : 128 * j] = -dot_nn(inverse, dot_nn(left, x[: 128 * j, : 128 * j]))
        product = dot_nt(f[:, : 128 * (j + 1)], x[here, : 128 * (j + 1)])
        for a in range(7):
            for b in range(7):
                r = 8 * (7 * a + b)
                out[a, b, :, here] = product[r : r + 7, :]
        if j < 3:
            x[here, 128 * (j + 1) :] = jnp.zeros((128, 512 - 128 * (j + 1)), jnp.float32)


def finish_call(packed, field, node_total):
    return pl.pallas_call(
        functools.partial(finish_kernel, node_total),
        out_shape=jax.ShapeDtypeStruct((7, 7, 7, 512), jnp.float32),
        in_specs=[pl.BlockSpec(memory_space=pltpu.VMEM)] * 2,
        out_specs=pl.BlockSpec(memory_space=pltpu.VMEM),
        scratch_shapes=[
            pltpu.VMEM((512, 512), jnp.float32),
            pltpu.VMEM((512, 512), jnp.float32),
            pltpu.VMEM((392, 512), jnp.float32),
        ],
        compiler_params=pltpu.CompilerParams(vmem_limit_bytes=40 << 20),
    )(packed, field)


band_low = 4.0
band_high = 34.0
anchor = 0.0


def extended_2(cells, sides, width):
    for axis, dim in sides:
        count = lax.axis_size(axis)
        head = lax.slice_in_dim(cells, 0, width, axis=dim)
        tail = lax.slice_in_dim(cells, cells.shape[dim] - width, cells.shape[dim], axis=dim)
        cells = jnp.concatenate(
            [
                lax.ppermute(tail, axis, [(i, (i + 1) % count) for i in range(count)]),
                cells,
                lax.ppermute(head, axis, [((i + 1) % count, i) for i in range(count)]),
            ],
            axis=dim,
        )
    return cells


def shifted_2(block, axis, distance):
    devices = range(lax.axis_size(axis))
    route = [((i - distance) % len(devices), i) for i in devices]
    return lax.ppermute(block, axis, route)


def fold_faces(padded, axis_pos):
    inner = lax.slice_in_dim(padded, 1, padded.shape[axis_pos] - 1, axis=axis_pos)
    count = inner.shape[axis_pos]
    first_plane = lax.slice_in_dim(inner, 0, 1, axis=axis_pos) + lax.slice_in_dim(
        padded, 0, 1, axis=axis_pos
    )
    middle = lax.slice_in_dim(inner, 1, count - 1, axis=axis_pos)
    last_plane = lax.slice_in_dim(inner, count - 1, count, axis=axis_pos) + lax.slice_in_dim(
        padded, count + 1, count + 2, axis=axis_pos
    )
    return jnp.concatenate([first_plane, middle, last_plane], axis=axis_pos)


def face_sum(partial_value):
    padded = extended_2(partial_value, (("wide", 0),), 1)
    folded = fold_faces(padded, 0)
    padded = extended_2(folded, (("narrow", 1),), 1)
    return fold_faces(padded, 1)


def final_sum(partial_value, order_now):
    return face_sum(partial_value)[:order_now, :order_now]


def apply_cells(fields, permuted, order_now, cells_here):
    edge = order_now + 1
    z_nodes = fields.shape[2]
    width = fields.shape[3]
    wrapped = jnp.concatenate([fields, fields[:, :, :1]], axis=2)
    inner_part = wrapped[:, :, :z_nodes].reshape(edge, edge, cells_here, order_now, width)
    tail_plane = wrapped[:, :, order_now::order_now][:, :, :, None]
    cell_boxes = jnp.concatenate([inner_part, tail_plane], axis=3).astype(jnp.bfloat16)
    products = jnp.einsum(
        "ckxyz,xyczn->ckn", permuted, cell_boxes, preferred_element_type=jnp.float32
    )
    products = products.reshape(cells_here, edge, edge, edge, width)
    body_part = products[:, :, :, :order_now]
    shifted = jnp.roll(products[:, :, :, order_now], 1, axis=0)
    combined = jnp.concatenate(
        [body_part[:, :, :, :1] + shifted[:, :, :, None], body_part[:, :, :, 1:]], axis=3
    )
    assembled = jnp.transpose(combined, (1, 2, 0, 3, 4))
    return assembled.reshape(edge, edge, z_nodes, width)


def on_device(orbitals, cell_matrix, cell_order):
    order_now = orbitals.shape[0]
    edge = order_now + 1
    width = orbitals.shape[3]
    matrices = cell_matrix[0, 0]
    ordering = cell_order[0, 0]
    cells_here = matrices.shape[0]
    inverse_order = jnp.argsort(ordering, axis=-1)
    permuted = jnp.take_along_axis(matrices, inverse_order[:, :, None], axis=1)
    permuted = jnp.take_along_axis(permuted, inverse_order[:, None, :], axis=2)
    permuted = permuted.reshape(cells_here, edge**3, edge, edge, edge)
    row_next = shifted_2(orbitals[:1], "wide", -1)
    extended = jnp.concatenate([orbitals, row_next], axis=0)
    column_next = shifted_2(extended[:, :1], "narrow", -1)
    current = jnp.concatenate([extended, column_next], axis=1)
    center = (band_low + band_high) / 2.0
    half_width = (band_high - band_low) / 2.0
    sigma_now = half_width / (anchor - center)
    tau_value = 2.0 / sigma_now
    previous = current
    for degree_step in range(DEG):
        final_apply = degree_step == DEG - 1
        image = apply_cells(current, permuted, order_now, cells_here)
        if final_apply:
            image = final_sum(image, order_now)
            current_part = current[:order_now, :order_now]
            previous_part = previous[:order_now, :order_now]
        else:
            image = face_sum(image)
            current_part = current
            previous_part = previous
        if degree_step == 0:
            updated = (image - center * current_part) * (sigma_now / half_width)
        else:
            sigma_new = 1.0 / (tau_value - sigma_now)
            updated = (image - center * current_part) * (
                2.0 * sigma_new / half_width
            ) - sigma_now * sigma_new * previous_part
            sigma_now = sigma_new
        previous, current = (current, updated)
    flattened = current.reshape(-1, width)
    node_total = flattened.shape[0] * lax.axis_size("wide") * lax.axis_size("narrow")
    local_correlation = jnp.einsum(
        "kn,km->nm", flattened, flattened, precision=lax.Precision.HIGHEST
    )
    packed = jnp.concatenate(
        [
            local_correlation[128 * i : 128 * i + 128, 128 * j : 128 * j + 128]
            for i in range(4)
            for j in range(i + 1)
        ],
        axis=0,
    ).reshape(TILES, 8, 128)
    total = ar_call(packed)
    return finish_call(total, current, node_total)


def solution(mesh):
    return jax.shard_map(
        on_device,
        mesh=mesh,
        in_specs=(
            P("wide", "narrow", None, None),
            P("wide", "narrow", None, None, None),
            P("wide", "narrow", None, None),
        ),
        out_specs=P("wide", "narrow", None, None),
        check_vma=False,
    )
```

```python
import functools

import jax
import jax.numpy as jnp
from jax import lax
from jax.experimental import pallas as pl
from jax.experimental.pallas import tpu as pltpu
from jax.sharding import PartitionSpec as P

MESH=pl.DeviceIdType.MESH
XS,YS,ZS=4,8,8
TILES=160
HALF=TILES//2
CA=HALF//XS
CB=3

def place():
    w=lax.axis_index("wide"); z=lax.axis_index("narrow")
    x=w//16; y=(w//2)%8; core=w%2
    return x,y,z,core

def at(x,y,z,core):
    return {"wide": x*16+y*2+core, "narrow": z}

def peers(x,y,z,core):
    out=[at(x,y,z,1-core)]
    for d in range(1,XS): out.append(at((x+d)%XS,y,z,core))
    for d in range(1,YS): out.append(at(x,(y+d)%YS,z,core))
    for d in range(1,ZS): out.append(at(x,y,(z+d)%ZS,core))
    return out

def ar_scratch():
    f=jnp.float32
    return [pltpu.VMEM((HALF,8,128),f),
            pltpu.VMEM((HALF,8,128),f),
            pltpu.VMEM((XS,CA,8,128),f),
            pltpu.VMEM((YS*CB,8,128),f),
            pltpu.VMEM((YS,CB,8,128),f),
            pltpu.VMEM((CB,8,128),f),
            pltpu.VMEM((ZS,CB,8,128),f),
            pltpu.VMEM((YS*CB,8,128),f),
            pltpu.SemaphoreType.DMA((40,)),
            pltpu.SemaphoreType.DMA((40,))]

def all_reduce(g, full, rc, acc, rx, sx, ry, sy, rz, gy, ssem, rsem):
    x,y,z,core=place()
    pend=[]
    cnt=[0]
    def send(src,dst,to):
        k=cnt[0]; cnt[0]+=1
        c=pltpu.make_async_remote_copy(src_ref=src,dst_ref=dst,send_sem=ssem.at[k],recv_sem=rsem.at[k],device_id=to,device_id_type=MESH)
        c.start(); pend.append(c)
        return c
    other=1-core
    c=send(g.at[pl.ds(other*HALF,HALF)],rc,at(x,y,z,other))
    c.wait_recv()
    acc[...]=g[pl.ds(core*HALF,HALF)]+rc[...]
    cs=[send(acc.at[pl.ds(((x+d)%XS)*CA,CA)],rx.at[d],at((x+d)%XS,y,z,core)) for d in range(1,XS)]
    for c in cs: c.wait_recv()
    s=acc[pl.ds(x*CA,CA)]
    for d in range(1,XS): s=s+rx[d]
    sx[0:CA]=s
    sx[CA:]=jnp.zeros((YS*CB-CA,8,128),jnp.float32)
    cs=[send(sx.at[pl.ds(((y+d)%YS)*CB,CB)],ry.at[d],at(x,(y+d)%YS,z,core)) for d in range(1,YS)]
    for c in cs: c.wait_recv()
    s=sx[pl.ds(y*CB,CB)]
    for d in range(1,YS): s=s+ry[d]
    sy[...]=s
    cs=[send(sy,rz.at[d],at(x,y,(z+d)%ZS,core)) for d in range(1,ZS)]
    for c in cs: c.wait_recv()
    for d in range(1,ZS): s=s+rz[d]
    gy[pl.ds(y*CB,CB)]=s
    cs=[send(gy.at[pl.ds(y*CB,CB)],gy.at[pl.ds(y*CB,CB)],at(x,(y+d)%YS,z,core)) for d in range(1,YS)]
    for c in cs: c.wait_recv()
    mine=core*HALF+x*CA
    full[pl.ds(mine,CA)]=gy[0:CA]
    cs=[send(gy.at[pl.ds(0,CA)],full.at[pl.ds(mine,CA)],at((x+d)%XS,y,z,core)) for d in range(1,XS)]
    f0=send(gy.at[pl.ds(0,CA)],full.at[pl.ds(mine,CA)],at(x,y,z,other))
    fs=[f0]
    for d in range(1,XS):
        cs[d-1].wait_recv()
        src=core*HALF+((x-d+XS)%XS)*CA
        fs.append(send(full.at[pl.ds(src,CA)],full.at[pl.ds(src,CA)],at(x,y,z,other)))
    for c in fs: c.wait_recv()
    for c in pend: c.wait_send()

def barrier(ps):
    sem=pltpu.get_barrier_semaphore()
    for p in ps: pl.semaphore_signal(sem,inc=1,device_id=p,device_id_type=MESH)
    pl.semaphore_wait(sem,len(ps))


DEG = 4
BAND_LOW = 4.0
BAND_HIGH = 34.0
ANCHOR = 0.0
WIDE, NARROW = XS * YS * 2, ZS
PART = 2
COLS = 512 // PART


def coefficients():
    center = (BAND_LOW + BAND_HIGH) / 2.0
    half = (BAND_HIGH - BAND_LOW) / 2.0
    sigma = half / (ANCHOR - center)
    tau = 2.0 / sigma
    out = [(sigma / half, 0.0)]
    for _ in range(DEG - 1):
        fresh = 1.0 / (tau - sigma)
        out.append((2.0 * fresh / half, sigma * fresh))
        sigma = fresh
    return center, out


def filter_scratch():
    f = jnp.float32
    return [
        pltpu.VMEM((512, 512), jnp.bfloat16),
        pltpu.VMEM((DEG, PART, 8, 8, 8, COLS), f),
        pltpu.VMEM((DEG, PART, 8, 8, 8, COLS), f),
        pltpu.VMEM((DEG, PART, 2, 8, 8, COLS), f),
        pltpu.VMEM((DEG, PART, 2, 8, 8, COLS), f),
        pltpu.VMEM((DEG, PART, 2, 2, 8, COLS), f),
        pltpu.SemaphoreType.DMA((DEG + 1, PART, 8)),
        pltpu.SemaphoreType.DMA((DEG + 1, PART, 8)),
    ]


def filter_steps(orbitals, matrix, order, field, mat, ys, zs, fw, fn, ce, ssem, rsem):
    w = lax.axis_index("wide")
    n = lax.axis_index("narrow")
    wn, wp = (w + 1) % WIDE, (w + WIDE - 1) % WIDE
    nn, np_ = (n + 1) % NARROW, (n + NARROW - 1) % NARROW
    center, weights = coefficients()
    pend = []

    def send(src, dst, r, h, k, to):
        c = pltpu.make_async_remote_copy(
            src_ref=src,
            dst_ref=dst,
            send_sem=ssem.at[r, h, k],
            recv_sem=rsem.at[r, h, k],
            device_id={"wide": to[0], "narrow": to[1]},
            device_id_type=MESH,
        )
        c.start()
        pend.append(c)
        return c

    copies = {}
    for h in range(PART):
        cols = slice(COLS * h, COLS * h + COLS)
        for i in range(7):
            for j in range(7):
                ys[0, h, i, j, 0:7] = orbitals[i, j, :, cols]
                ys[0, h, i, j, 7:8] = orbitals[i, j, 0:1, cols]
        y = ys.at[0, h]
        copies[0, h] = [
            send(y.at[0, 0:7], y.at[7, 0:7], 0, h, 0, (wp, n)),
            send(y.at[0:7, 0], y.at[0:7, 7], 0, h, 1, (w, np_)),
            send(y.at[0, 0], y.at[7, 7], 0, h, 2, (wp, np_)),
        ]
    place_of = jnp.where(
        lax.broadcasted_iota(jnp.int32, (512, 512), 0) == jnp.broadcast_to(order[...], (512, 512)), 1.0, 0.0
    ).astype(jnp.bfloat16)
    rows_placed = jnp.dot(place_of, matrix[...], preferred_element_type=jnp.float32).astype(jnp.bfloat16)
    mat[...] = lax.dot_general(
        rows_placed, place_of, (((1,), (1,)), ((), ())), preferred_element_type=jnp.float32
    ).astype(jnp.bfloat16)

    sub = lax.broadcasted_iota(jnp.int32, (8, 8, COLS), 1)

    def updated(image, r, h, i, j):
        out = (image - center * ys[r, h, i, j]) * weights[r][0]
        if r > 0:
            out = out - weights[r][1] * ys[r - 1, h, i, j]
        return out

    def store(r, h, i, j, value):
        if r < DEG - 1:
            ys[r + 1, h, i, j] = value
        elif not isinstance(i, int) or i < 7:
            field[h, i, j] = value

    def interior(r, h):
        inner = slice(1, 7)
        for i in range(1, 7):
            value = updated(zs[r, h, i, inner], r, h, i, inner)
            if r == DEG - 1:
                value = jnp.where(sub[1:7] < 7, value, 0.0)
            store(r, h, i, inner, value)

    def border(r, h):
        last = r == DEG - 1
        keep = (lambda v: jnp.where(sub[0, :, :] < 7, v, 0.0)) if last else (lambda v: v)
        for i in range(7 if last else 8):
            edge = i in (0, 7)
            for j in range(8) if edge else (0, 7):
                if last and j == 7:
                    field[h, i, 7] = jnp.zeros((8, COLS), jnp.float32)
                    continue
                image = zs[r, h, i, j]
                a, b = (0 if i == 0 else 1), (0 if j == 0 else 1)
                if edge:
                    image = image + fw[r, h, a, j]
                if j in (0, 7):
                    image = image + fn[r, h, b, i]
                    if edge:
                        image = image + ce[r, h, a, b]
                store(r, h, i, j, keep(updated(image, r, h, i, j)))

    for r in range(DEG):
        for h in range(PART):
            for c in copies[r, h]:
                c.wait_recv()
            if r > 0:
                border(r - 1, h)
            rounded = ys[r, h].reshape(512, COLS).astype(jnp.bfloat16)
            product = jnp.dot(mat[...], rounded, preferred_element_type=jnp.float32).reshape(8, 8, 8, COLS)
            for i in range(8):
                v = product[i]
                joined = jnp.where(
                    sub == 0, pltpu.roll(v, 1, axis=1), jnp.where(sub == 7, pltpu.roll(v, 7, axis=1), 0.0)
                )
                zs[r, h, i] = v + joined
            z, gw, gn, gc = zs.at[r, h], fw.at[r, h], fn.at[r, h], ce.at[r, h]
            cs = [
                send(z.at[7], gw.at[0], r + 1, h, 0, (wn, n)),
                send(z.at[:, 7], gn.at[0], r + 1, h, 1, (w, nn)),
                send(z.at[7, 7], gc.at[0, 0], r + 1, h, 2, (wn, nn)),
            ]
            if r < DEG - 1:
                cs += [
                    send(z.at[0], gw.at[1], r + 1, h, 3, (wp, n)),
                    send(z.at[:, 0], gn.at[1], r + 1, h, 4, (w, np_)),
                    send(z.at[7, 0], gc.at[0, 1], r + 1, h, 5, (wn, np_)),
                    send(z.at[0, 7], gc.at[1, 0], r + 1, h, 6, (wp, nn)),
                    send(z.at[0, 0], gc.at[1, 1], r + 1, h, 7, (wp, np_)),
                ]
            copies[r + 1, h] = cs
            interior(r, h)
    for h in range(PART):
        for c in copies[DEG, h]:
            c.wait_recv()
        border(DEG - 1, h)
    return pend


def neighbours(w, n):
    return [
        {"wide": (w + a) % WIDE, "narrow": (n + b) % NARROW}
        for a in (WIDE - 1, 0, 1)
        for b in (NARROW - 1, 0, 1)
        if (a, b) != (0, 0)
    ]


def gram_tiles(field, tiles):
    def dot_tn(a, b):
        return lax.dot_general(
            a, b, (((0,), (0,)), ((), ())), precision=lax.Precision.HIGHEST, preferred_element_type=jnp.float32
        )

    cols = [field[h].reshape(448, COLS) for h in range(PART)]
    per = COLS // 128
    for a in range(PART):
        for b in range(a + 1):
            block = dot_tn(cols[a], cols[b])
            for i in range(per):
                for j in range(per):
                    p, q = a * per + i, b * per + j
                    if q <= p:
                        t = 16 * (p * (p + 1) // 2 + q)
                        tiles[t : t + 16] = block[128 * i : 128 * i + 128, 128 * j : 128 * j + 128].reshape(16, 8, 128)


def filter_kernel(orbitals, matrix, order, field, full, tiles, *scratch):
    barrier(neighbours(lax.axis_index("wide"), lax.axis_index("narrow")) + peers(*place()))
    pend = filter_steps(orbitals, matrix, order, field, *scratch[:8])
    gram_tiles(field, tiles)
    all_reduce(tiles, full, *scratch[8:])
    for c in pend:
        c.wait_send()


def filter_call(orbitals, matrix, order):
    return pl.pallas_call(
        filter_kernel,
        out_shape=(
            jax.ShapeDtypeStruct((PART, 7, 8, 8, COLS), jnp.float32),
            jax.ShapeDtypeStruct((TILES, 8, 128), jnp.float32),
        ),
        in_specs=[pl.BlockSpec(memory_space=pltpu.VMEM)] * 3,
        out_specs=[pl.BlockSpec(memory_space=pltpu.VMEM)] * 2,
        scratch_shapes=[pltpu.VMEM((TILES, 8, 128), jnp.float32)] + filter_scratch() + ar_scratch(),
        compiler_params=pltpu.CompilerParams(collective_id=0, has_side_effects=True, vmem_limit_bytes=48 << 20),
    )(orbitals, matrix, order)


def dot_nn(a, b):
    return lax.dot_general(
        a, b, (((1,), (0,)), ((), ())), precision=lax.Precision.HIGHEST, preferred_element_type=jnp.float32
    )


def dot_nt(a, b):
    return lax.dot_general(
        a, b, (((1,), (1,)), ((), ())), precision=lax.Precision.HIGHEST, preferred_element_type=jnp.float32
    )


def reciprocal(d):
    r = pl.reciprocal(d, approx=True)
    r = r * (2.0 - d * r)
    return r * (2.0 - d * r)


def inverse_factor(block):
    rows = [block[8 * i : 8 * i + 8, :] for i in range(16)]
    lane = lax.broadcasted_iota(jnp.int32, (8, 128), 1)
    sub = lax.broadcasted_iota(jnp.int32, (8, 128), 0)
    for b in range(16):
        first = 8 * b
        panel = [jnp.broadcast_to(rows[b][i : i + 1, :], (8, 128)) for i in range(8)]
        e = {}
        for i in range(8):
            for j in range(i, 8):
                e[i, j] = jnp.broadcast_to(panel[i][:, first + j : first + j + 1], (8, 128))
        inside = (lane >= first) & (lane < first + 8)
        p = [jnp.where(inside, jnp.where(lane == first + i, 1.0, 0.0), panel[i]) for i in range(8)]
        inv = [None] * 8
        m = {}
        for k in range(8):
            inv[k] = reciprocal(e[k, k])
            for i in range(k + 1, 8):
                m[i, k] = e[k, i] * inv[k]
                for j in range(i, 8):
                    e[i, j] = e[i, j] - m[i, k] * e[k, j]
                p[i] = p[i] - m[i, k] * p[k]
        if b < 15:
            s = [p[k] * inv[k] for k in range(8)]
            for l in range(6, -1, -1):
                for k in range(7, l, -1):
                    s[l] = s[l] - m[k, l] * s[k]
            for i in range(b + 1, 16):
                below = rows[i]
                total = jnp.where(inside, 0.0, below)
                for k in range(8):
                    total = total - jnp.broadcast_to(below[:, first + k : first + k + 1], (8, 128)) * s[k]
                rows[i] = total
        own, pivot = p[0], e[0, 0]
        for k in range(1, 8):
            own = jnp.where(sub == k, p[k], own)
            pivot = jnp.where(sub == k, e[k, k], pivot)
        y = lax.rsqrt(pivot)
        y = y * (1.5 - 0.5 * pivot * y * y)
        rows[b] = jnp.where(lane <= sub + first, own, 0.0) * y
    return jnp.concatenate(rows, axis=0)


def finish_kernel(node_total, packed, field, out, w, x, f):
    for i in range(4):
        for j in range(i + 1):
            at_tile = 16 * (i * (i + 1) // 2 + j)
            w[128 * i : 128 * i + 128, 128 * j : 128 * j + 128] = (
                packed[at_tile : at_tile + 16].reshape(128, 128) * (1.0 / node_total)
            )
    for h in range(PART):
        f[:, COLS * h : COLS * h + COLS] = field[h].reshape(448, COLS)
    lower = {}
    for j in range(4):
        here = slice(128 * j, 128 * j + 128)
        inverse = inverse_factor(w[here, here])
        if j < 3:
            column = dot_nt(w[128 * (j + 1) :, here], inverse)
            lower[j] = column
            for i in range(j + 1, 4):
                band = column[128 * (i - j - 1) : 128 * (i - j)]
                w[128 * i : 128 * i + 128, 128 * (j + 1) : 128 * (i + 1)] = w[
                    128 * i : 128 * i + 128, 128 * (j + 1) : 128 * (i + 1)
                ] - dot_nt(band, column[: 128 * (i - j)])
        x[here, here] = inverse
        if j > 0:
            left = jnp.concatenate([lower[k][128 * (j - k - 1) : 128 * (j - k)] for k in range(j)], axis=1)
            x[here, : 128 * j] = -dot_nn(inverse, dot_nn(left, x[: 128 * j, : 128 * j]))
        product = dot_nt(f[:, : 128 * (j + 1)], x[here, : 128 * (j + 1)])
        for a in range(7):
            for b in range(7):
                r = 64 * a + 8 * b
                out[a, b, :, here] = product[r : r + 7, :]
        if j < 3:
            x[here, 128 * (j + 1) :] = jnp.zeros((128, 512 - 128 * (j + 1)), jnp.float32)


def finish_call(packed, field, node_total):
    return pl.pallas_call(
        functools.partial(finish_kernel, node_total),
        out_shape=jax.ShapeDtypeStruct((7, 7, 7, 512), jnp.float32),
        in_specs=[pl.BlockSpec(memory_space=pltpu.VMEM)] * 2,
        out_specs=pl.BlockSpec(memory_space=pltpu.VMEM),
        scratch_shapes=[
            pltpu.VMEM((512, 512), jnp.float32),
            pltpu.VMEM((512, 512), jnp.float32),
            pltpu.VMEM((448, 512), jnp.float32),
        ],
        compiler_params=pltpu.CompilerParams(vmem_limit_bytes=40 << 20),
    )(packed, field)


def on_device(orbitals, cell_matrix, cell_order):
    node_total = 343.0 * WIDE * NARROW
    field, total = filter_call(orbitals, cell_matrix.reshape(512, 512), cell_order.reshape(1, 512))
    return finish_call(total, field, node_total)


def solution(mesh):
    return jax.shard_map(
        on_device,
        mesh=mesh,
        in_specs=(
            P("wide", "narrow", None, None),
            P("wide", "narrow", None, None, None),
            P("wide", "narrow", None, None),
        ),
        out_specs=P("wide", "narrow", None, None),
        check_vma=False,
    )
```

```python
import functools

import jax
import jax.numpy as jnp
from jax import lax
from jax.experimental import pallas as pl
from jax.experimental.pallas import tpu as pltpu
from jax.sharding import PartitionSpec as P

MESH=pl.DeviceIdType.MESH
XS,YS,ZS=4,8,8
TILES=160
HALF=TILES//2
CA=HALF//XS
CB=3

def place():
    w=lax.axis_index("wide"); z=lax.axis_index("narrow")
    x=w//16; y=(w//2)%8; core=w%2
    return x,y,z,core

def at(x,y,z,core):
    return {"wide": x*16+y*2+core, "narrow": z}

def peers(x,y,z,core):
    out=[at(x,y,z,1-core)]
    for d in range(1,XS): out.append(at((x+d)%XS,y,z,core))
    for d in range(1,YS): out.append(at(x,(y+d)%YS,z,core))
    for d in range(1,ZS): out.append(at(x,y,(z+d)%ZS,core))
    return out

def ar_scratch():
    f=jnp.float32
    return [pltpu.VMEM((HALF,8,128),f),
            pltpu.VMEM((HALF,8,128),f),
            pltpu.VMEM((XS,CA,8,128),f),
            pltpu.VMEM((YS*CB,8,128),f),
            pltpu.VMEM((YS,CB,8,128),f),
            pltpu.VMEM((CB,8,128),f),
            pltpu.VMEM((ZS,CB,8,128),f),
            pltpu.VMEM((YS*CB,8,128),f),
            pltpu.SemaphoreType.DMA((40,)),
            pltpu.SemaphoreType.DMA((40,))]

def all_reduce(g, full, rc, acc, rx, sx, ry, sy, rz, gy, ssem, rsem):
    x,y,z,core=place()
    pend=[]
    cnt=[0]
    def send(src,dst,to):
        k=cnt[0]; cnt[0]+=1
        c=pltpu.make_async_remote_copy(src_ref=src,dst_ref=dst,send_sem=ssem.at[k],recv_sem=rsem.at[k],device_id=to,device_id_type=MESH)
        c.start(); pend.append(c)
        return c
    other=1-core
    c=send(g.at[pl.ds(other*HALF,HALF)],rc,at(x,y,z,other))
    c.wait_recv()
    acc[...]=g[pl.ds(core*HALF,HALF)]+rc[...]
    cs=[send(acc.at[pl.ds(((x+d)%XS)*CA,CA)],rx.at[d],at((x+d)%XS,y,z,core)) for d in range(1,XS)]
    for c in cs: c.wait_recv()
    s=acc[pl.ds(x*CA,CA)]
    for d in range(1,XS): s=s+rx[d]
    sx[0:CA]=s
    sx[CA:]=jnp.zeros((YS*CB-CA,8,128),jnp.float32)
    cs=[send(sx.at[pl.ds(((y+d)%YS)*CB,CB)],ry.at[d],at(x,(y+d)%YS,z,core)) for d in range(1,YS)]
    for c in cs: c.wait_recv()
    s=sx[pl.ds(y*CB,CB)]
    for d in range(1,YS): s=s+ry[d]
    sy[...]=s
    cs=[send(sy,rz.at[d],at(x,y,(z+d)%ZS,core)) for d in range(1,ZS)]
    for c in cs: c.wait_recv()
    for d in range(1,ZS): s=s+rz[d]
    gy[pl.ds(y*CB,CB)]=s
    cs=[send(gy.at[pl.ds(y*CB,CB)],gy.at[pl.ds(y*CB,CB)],at(x,(y+d)%YS,z,core)) for d in range(1,YS)]
    for c in cs: c.wait_recv()
    mine=core*HALF+x*CA
    full[pl.ds(mine,CA)]=gy[0:CA]
    cs=[send(gy.at[pl.ds(0,CA)],full.at[pl.ds(mine,CA)],at((x+d)%XS,y,z,core)) for d in range(1,XS)]
    f0=send(gy.at[pl.ds(0,CA)],full.at[pl.ds(mine,CA)],at(x,y,z,other))
    fs=[f0]
    for d in range(1,XS):
        cs[d-1].wait_recv()
        src=core*HALF+((x-d+XS)%XS)*CA
        fs.append(send(full.at[pl.ds(src,CA)],full.at[pl.ds(src,CA)],at(x,y,z,other)))
    for c in fs: c.wait_recv()
    for c in pend: c.wait_send()

def barrier(ps):
    sem=pltpu.get_barrier_semaphore()
    for p in ps: pl.semaphore_signal(sem,inc=1,device_id=p,device_id_type=MESH)
    pl.semaphore_wait(sem,len(ps))


DEG = 4
BAND_LOW = 4.0
BAND_HIGH = 34.0
ANCHOR = 0.0
WIDE, NARROW = XS * YS * 2, ZS
PART = 2
COLS = 512 // PART


def coefficients():
    center = (BAND_LOW + BAND_HIGH) / 2.0
    half = (BAND_HIGH - BAND_LOW) / 2.0
    sigma = half / (ANCHOR - center)
    tau = 2.0 / sigma
    out = [(sigma / half, 0.0)]
    for _ in range(DEG - 1):
        fresh = 1.0 / (tau - sigma)
        out.append((2.0 * fresh / half, sigma * fresh))
        sigma = fresh
    return center, out


def filter_scratch():
    f = jnp.float32
    return [
        pltpu.VMEM((512, 512), jnp.bfloat16),
        pltpu.VMEM((DEG, PART, 8, 8, 8, COLS), f),
        pltpu.VMEM((DEG, PART, 8, 8, 8, COLS), f),
        pltpu.VMEM((DEG, PART, 2, 8, 8, COLS), f),
        pltpu.VMEM((DEG, PART, 2, 8, 8, COLS), f),
        pltpu.VMEM((DEG, PART, 2, 2, 8, COLS), f),
        pltpu.SemaphoreType.DMA((DEG + 1, PART, 8)),
        pltpu.SemaphoreType.DMA((DEG + 1, PART, 8)),
    ]


def filter_steps(loads, matrix, order, field, mat, ys, zs, fw, fn, ce, ssem, rsem):
    w = lax.axis_index("wide")
    n = lax.axis_index("narrow")
    wn, wp = (w + 1) % WIDE, (w + WIDE - 1) % WIDE
    nn, np_ = (n + 1) % NARROW, (n + NARROW - 1) % NARROW
    center, weights = coefficients()
    pend = []

    def send(src, dst, r, h, k, to):
        c = pltpu.make_async_remote_copy(
            src_ref=src,
            dst_ref=dst,
            send_sem=ssem.at[r, h, k],
            recv_sem=rsem.at[r, h, k],
            device_id={"wide": to[0], "narrow": to[1]},
            device_id_type=MESH,
        )
        c.start()
        pend.append(c)
        return c

    copies = {}
    for h in range(PART):
        loads[1 + h].wait()
        for i in range(7):
            for j in range(7):
                ys[0, h, i, j, 7:8] = ys[0, h, i, j, 0:1]
        y = ys.at[0, h]
        copies[0, h] = [
            send(y.at[0, 0], y.at[7, 7], 0, h, 2, (wp, np_)),
            send(y.at[0:7, 0], y.at[0:7, 7], 0, h, 1, (w, np_)),
            send(y.at[0, 0:7], y.at[7, 0:7], 0, h, 0, (wp, n)),
        ]
    loads[0].wait()
    place_of = jnp.where(
        lax.broadcasted_iota(jnp.int32, (512, 512), 0) == jnp.broadcast_to(order[...], (512, 512)), 1.0, 0.0
    ).astype(jnp.bfloat16)
    rows_placed = jnp.dot(place_of, matrix[...], preferred_element_type=jnp.float32).astype(jnp.bfloat16)
    mat[...] = lax.dot_general(
        rows_placed, place_of, (((1,), (1,)), ((), ())), preferred_element_type=jnp.float32
    ).astype(jnp.bfloat16)

    sub = lax.broadcasted_iota(jnp.int32, (8, 8, COLS), 1)

    def updated(image, r, h, i, j):
        out = (image - center * ys[r, h, i, j]) * weights[r][0]
        if r > 0:
            out = out - weights[r][1] * ys[r - 1, h, i, j]
        return out

    def store(r, h, i, j, value):
        if r < DEG - 1:
            ys[r + 1, h, i, j] = value
        elif not isinstance(i, int) or i < 7:
            field[h, i, j] = value

    def interior(r, h):
        inner = slice(1, 7)
        for i in range(1, 7):
            value = updated(zs[r, h, i, inner], r, h, i, inner)
            if r == DEG - 1:
                value = jnp.where(sub[1:7] < 7, value, 0.0)
            store(r, h, i, inner, value)

    def border(r, h):
        last = r == DEG - 1
        keep = (lambda v: jnp.where(sub[0, :, :] < 7, v, 0.0)) if last else (lambda v: v)
        for i in range(7 if last else 8):
            edge = i in (0, 7)
            for j in range(8) if edge else (0, 7):
                if last and j == 7:
                    field[h, i, 7] = jnp.zeros((8, COLS), jnp.float32)
                    continue
                image = zs[r, h, i, j]
                a, b = (0 if i == 0 else 1), (0 if j == 0 else 1)
                if edge:
                    image = image + fw[r, h, a, j]
                if j in (0, 7):
                    image = image + fn[r, h, b, i]
                    if edge:
                        image = image + ce[r, h, a, b]
                store(r, h, i, j, keep(updated(image, r, h, i, j)))

    for r in range(DEG):
        for h in range(PART):
            for c in copies[r, h]:
                c.wait_recv()
            if r > 0:
                border(r - 1, h)
            rounded = ys[r, h].reshape(512, COLS).astype(jnp.bfloat16)
            product = jnp.dot(mat[...], rounded, preferred_element_type=jnp.float32).reshape(8, 8, 8, COLS)
            for i in range(8):
                v = product[i]
                joined = jnp.where(
                    sub == 0, pltpu.roll(v, 1, axis=1), jnp.where(sub == 7, pltpu.roll(v, 7, axis=1), 0.0)
                )
                zs[r, h, i] = v + joined
            z, gw, gn, gc = zs.at[r, h], fw.at[r, h], fn.at[r, h], ce.at[r, h]
            both = r < DEG - 1
            cs = [send(z.at[7, 7], gc.at[0, 0], r + 1, h, 2, (wn, nn))]
            if both:
                cs += [
                    send(z.at[0, 0], gc.at[1, 1], r + 1, h, 7, (wp, np_)),
                    send(z.at[7, 0], gc.at[0, 1], r + 1, h, 5, (wn, np_)),
                    send(z.at[0, 7], gc.at[1, 0], r + 1, h, 6, (wp, nn)),
                ]
            cs.append(send(z.at[:, 7], gn.at[0], r + 1, h, 1, (w, nn)))
            if both:
                cs.append(send(z.at[:, 0], gn.at[1], r + 1, h, 4, (w, np_)))
            cs.append(send(z.at[7], gw.at[0], r + 1, h, 0, (wn, n)))
            if both:
                cs.append(send(z.at[0], gw.at[1], r + 1, h, 3, (wp, n)))
            copies[r + 1, h] = cs
            interior(r, h)
    for h in range(PART):
        for c in copies[DEG, h]:
            c.wait_recv()
        border(DEG - 1, h)
    return pend


def neighbours(w, n):
    return [
        {"wide": (w + a) % WIDE, "narrow": (n + b) % NARROW}
        for a in (WIDE - 1, 0, 1)
        for b in (NARROW - 1, 0, 1)
        if (a, b) != (0, 0)
    ]


def gram_tiles(field, tiles):
    def dot_tn(a, b):
        return lax.dot_general(
            a, b, (((0,), (0,)), ((), ())), precision=lax.Precision.HIGHEST, preferred_element_type=jnp.float32
        )

    cols = [field[h].reshape(448, COLS) for h in range(PART)]
    per = COLS // 128
    for a in range(PART):
        for b in range(a + 1):
            block = dot_tn(cols[a], cols[b])
            for i in range(per):
                for j in range(per):
                    p, q = a * per + i, b * per + j
                    if q <= p:
                        t = 16 * (p * (p + 1) // 2 + q)
                        tiles[t : t + 16] = block[128 * i : 128 * i + 128, 128 * j : 128 * j + 128].reshape(16, 8, 128)


def filter_kernel(orbitals, matrix, order, field, full, tiles, held, lsem, *scratch):
    ys = scratch[1]
    loads = [pltpu.make_async_copy(matrix, held, lsem.at[0])] + [
        pltpu.make_async_copy(
            orbitals.at[:, :, :, COLS * h : COLS * h + COLS], ys.at[0, h, 0:7, 0:7, 0:7], lsem.at[1 + h]
        )
        for h in range(PART)
    ]
    for c in loads[1:] + loads[:1]:
        c.start()
    barrier(neighbours(lax.axis_index("wide"), lax.axis_index("narrow")) + peers(*place()))
    pend = filter_steps(loads, held, order, field, *scratch[:8])
    gram_tiles(field, tiles)
    all_reduce(tiles, full, *scratch[8:])
    for c in pend:
        c.wait_send()


def filter_call(orbitals, matrix, order):
    return pl.pallas_call(
        filter_kernel,
        out_shape=(
            jax.ShapeDtypeStruct((PART, 7, 8, 8, COLS), jnp.float32),
            jax.ShapeDtypeStruct((TILES, 8, 128), jnp.float32),
        ),
        in_specs=[pl.BlockSpec(memory_space=pl.ANY)] * 2 + [pl.BlockSpec(memory_space=pltpu.VMEM)],
        out_specs=[pl.BlockSpec(memory_space=pltpu.VMEM)] * 2,
        scratch_shapes=[
            pltpu.VMEM((TILES, 8, 128), jnp.float32),
            pltpu.VMEM((512, 512), jnp.bfloat16),
            pltpu.SemaphoreType.DMA((1 + PART,)),
        ] + filter_scratch() + ar_scratch(),
        compiler_params=pltpu.CompilerParams(collective_id=0, has_side_effects=True, vmem_limit_bytes=48 << 20),
    )(orbitals, matrix, order)


def halves(a):
    high = a.astype(jnp.bfloat16)
    return high, (a - high.astype(jnp.float32)).astype(jnp.bfloat16)


def product(a, b, dims):
    (ah, al), (bh, bl) = halves(a), halves(b)

    def one(p, q):
        return lax.dot_general(p, q, (dims, ((), ())), preferred_element_type=jnp.float32)

    return one(ah, bh) + (one(ah, bl) + one(al, bh))


def dot_nn(a, b):
    return product(a, b, ((1,), (0,)))


def dot_nt(a, b):
    return product(a, b, ((1,), (1,)))


def reciprocal(d):
    r = pl.reciprocal(d, approx=True)
    return r * (2.0 - d * r)


def thirds(a):
    high = a.astype(jnp.bfloat16).astype(jnp.float32)
    rest = a - high
    middle = rest.astype(jnp.bfloat16).astype(jnp.float32)
    return high, middle, rest - middle


def outer(r, s):
    (rh, rm, rl), (sh, sm, sl) = thirds(r), thirds(s)
    left = jnp.concatenate([rh, rh, rm, rm, rh, rl], axis=0).astype(jnp.bfloat16)
    right = jnp.concatenate([sh, sm, sh, sm, sl, sh], axis=0).astype(jnp.bfloat16)
    return lax.dot_general(left, right, (((0,), (0,)), ((), ())), preferred_element_type=jnp.float32)


def inverse_factor(block):
    rows = [block[8 * i : 8 * i + 8, :] for i in range(16)]
    lane = lax.broadcasted_iota(jnp.int32, (8, 128), 1)
    sub = lax.broadcasted_iota(jnp.int32, (8, 128), 0)
    for b in range(16):
        first = 8 * b
        panel = [jnp.broadcast_to(rows[b][i : i + 1, :], (8, 128)) for i in range(8)]
        e = {}
        for i in range(8):
            for j in range(i, 8):
                e[i, j] = jnp.broadcast_to(panel[i][:, first + j : first + j + 1], (8, 128))
        inside = (lane >= first) & (lane < first + 8)
        p = [jnp.where(inside, jnp.where(lane == first + i, 1.0, 0.0), panel[i]) for i in range(8)]
        if b < 15:
            below = rows[b + 1]
            c = [jnp.broadcast_to(below[:, first + k : first + k + 1], (8, 128)) for k in range(8)]
        inv = [None] * 8
        m = {}
        for k in range(0, 8, 2):
            u, v, t = e[k, k], e[k, k + 1], e[k + 1, k + 1]
            det = u * t - v * v
            over = reciprocal(det)
            iu, iv, it = t * over, v * over, u * over
            inv[k] = reciprocal(u)
            inv[k + 1] = it
            m[k + 1, k] = v * inv[k]
            e[k + 1, k + 1] = det * inv[k]
            for i in range(k + 2, 8):
                f, g = e[k, i], e[k + 1, i]
                one, two = f * iu - g * iv, g * it - f * iv
                for j in range(i, 8):
                    e[i, j] = e[i, j] - (one * e[k, j] + two * e[k + 1, j])
                m[i, k], m[i, k + 1] = f * inv[k], two
            p[k + 1] = p[k + 1] - m[k + 1, k] * p[k]
            for i in range(k + 2, 8):
                p[i] = p[i] - (m[i, k] * p[k] + m[i, k + 1] * p[k + 1])
        own, pivot = p[0], e[0, 0]
        for k in range(1, 8):
            own = jnp.where(sub == k, p[k], own)
            pivot = jnp.where(sub == k, e[k, k], pivot)
        if b < 15:
            s = [p[k] * inv[k] for k in range(8)]
            for l in range(6, -1, -1):
                for k in range(7, l, -1):
                    s[l] = s[l] - m[k, l] * s[k]
            terms = [c[k] * s[k] for k in range(8)]
            while len(terms) > 1:
                terms = [terms[i] + terms[i + 1] for i in range(0, len(terms), 2)]
            fresh = jnp.where(inside, 0.0, below) - terms[0]
            if b < 14:
                change = outer(own, own * reciprocal(pivot))
                for i in range(b + 2, 16):
                    rows[i] = jnp.where(inside, 0.0, rows[i]) - change[8 * i : 8 * i + 8]
            rows[b + 1] = fresh
        y = lax.rsqrt(pivot)
        y = y * (1.5 - 0.5 * pivot * y * y)
        rows[b] = jnp.where(lane <= sub + first, own, 0.0) * y
    return jnp.concatenate(rows, axis=0)


def finish_kernel(node_total, packed, field, out, w, x, f):
    on_diagonal = lax.broadcasted_iota(jnp.int32, (128, 128), 0) == lax.broadcasted_iota(jnp.int32, (128, 128), 1)

    def block(i, j):
        at_tile = 16 * (i * (i + 1) // 2 + j)
        return packed[at_tile : at_tile + 16].reshape(128, 128) * (1.0 / node_total)

    scale_row, scale_column = [], []
    for i in range(4):
        diagonal = jnp.where(on_diagonal, block(i, i), 0.0)
        s = jnp.broadcast_to(lax.rsqrt(jnp.sum(diagonal, axis=0, keepdims=True)), (128, 128))
        scale_row.append(s)
        scale_column.append(jnp.broadcast_to(jnp.sum(jnp.where(on_diagonal, s, 0.0), axis=1, keepdims=True), (128, 128)))
    for i in range(4):
        for j in range(i + 1):
            w[128 * i : 128 * i + 128, 128 * j : 128 * j + 128] = block(i, j) * scale_column[i] * scale_row[j]
    for j in range(4):
        h, q = divmod(128 * j, COLS)
        cols = field[h].reshape(448, COLS)[:, q : q + 128]
        f[:, 128 * j : 128 * j + 128] = cols * scale_row[j][0:1, :]
    lower = {}
    for j in range(4):
        here = slice(128 * j, 128 * j + 128)
        inverse = inverse_factor(w[here, here])
        if j < 3:
            column = dot_nt(w[128 * (j + 1) :, here], inverse)
            lower[j] = column
            for i in range(j + 1, 4):
                band = column[128 * (i - j - 1) : 128 * (i - j)]
                w[128 * i : 128 * i + 128, 128 * (j + 1) : 128 * (i + 1)] = w[
                    128 * i : 128 * i + 128, 128 * (j + 1) : 128 * (i + 1)
                ] - dot_nt(band, column[: 128 * (i - j)])
        x[here, here] = inverse
        if j > 0:
            left = jnp.concatenate([lower[k][128 * (j - k - 1) : 128 * (j - k)] for k in range(j)], axis=1)
            x[here, : 128 * j] = -dot_nn(inverse, dot_nn(left, x[: 128 * j, : 128 * j]))
        rotated = dot_nt(f[:, : 128 * (j + 1)], x[here, : 128 * (j + 1)])
        for a in range(7):
            for b in range(7):
                r = 64 * a + 8 * b
                out[a, b, :, here] = rotated[r : r + 7, :]
        if j < 3:
            x[here, 128 * (j + 1) :] = jnp.zeros((128, 512 - 128 * (j + 1)), jnp.float32)


def finish_call(packed, field, node_total):
    return pl.pallas_call(
        functools.partial(finish_kernel, node_total),
        out_shape=jax.ShapeDtypeStruct((7, 7, 7, 512), jnp.float32),
        in_specs=[pl.BlockSpec(memory_space=pltpu.VMEM)] * 2,
        out_specs=pl.BlockSpec(memory_space=pltpu.VMEM),
        scratch_shapes=[
            pltpu.VMEM((512, 512), jnp.float32),
            pltpu.VMEM((512, 512), jnp.float32),
            pltpu.VMEM((448, 512), jnp.float32),
        ],
        compiler_params=pltpu.CompilerParams(vmem_limit_bytes=40 << 20),
    )(packed, field)


def on_device(orbitals, cell_matrix, cell_order):
    node_total = 343.0 * WIDE * NARROW
    field, total = filter_call(orbitals, cell_matrix.reshape(512, 512), cell_order.reshape(1, 512))
    return finish_call(total, field, node_total)


def solution(mesh):
    return jax.shard_map(
        on_device,
        mesh=mesh,
        in_specs=(
            P("wide", "narrow", None, None),
            P("wide", "narrow", None, None, None),
            P("wide", "narrow", None, None),
        ),
        out_specs=P("wide", "narrow", None, None),
        check_vma=False,
    )
```

```python
import functools

import jax
import jax.numpy as jnp
from jax import lax
from jax.experimental import pallas as pl
from jax.experimental.pallas import tpu as pltpu
from jax.sharding import PartitionSpec as P

MESH=pl.DeviceIdType.MESH
XS,YS,ZS=4,8,8
TILES=160
HALF=TILES//2
CA=HALF//XS
CB=3


def far_first(count):
    return sorted(range(1,count),key=lambda d:-min(d,count-d))

def place():
    w=lax.axis_index("wide"); z=lax.axis_index("narrow")
    x=w//16; y=(w//2)%8; core=w%2
    return x,y,z,core

def at(x,y,z,core):
    return {"wide": x*16+y*2+core, "narrow": z}

def peers(x,y,z,core):
    out=[at(x,y,z,1-core)]
    for d in range(1,XS): out.append(at((x+d)%XS,y,z,core))
    for d in range(1,YS): out.append(at(x,(y+d)%YS,z,core))
    for d in range(1,ZS): out.append(at(x,y,(z+d)%ZS,core))
    return out

def ar_scratch():
    f=jnp.float32
    return [pltpu.VMEM((HALF,8,128),f),
            pltpu.VMEM((HALF,8,128),f),
            pltpu.VMEM((XS,CA,8,128),f),
            pltpu.VMEM((YS*CB,8,128),f),
            pltpu.VMEM((YS,CB,8,128),f),
            pltpu.VMEM((CB,8,128),f),
            pltpu.VMEM((ZS,CB,8,128),f),
            pltpu.VMEM((YS*CB,8,128),f),
            pltpu.SemaphoreType.DMA((40,)),
            pltpu.SemaphoreType.DMA((40,))]

def all_reduce(g, full, rc, acc, rx, sx, ry, sy, rz, gy, ssem, rsem):
    x,y,z,core=place()
    pend=[]
    cnt=[0]
    def send(src,dst,to):
        k=cnt[0]; cnt[0]+=1
        c=pltpu.make_async_remote_copy(src_ref=src,dst_ref=dst,send_sem=ssem.at[k],recv_sem=rsem.at[k],device_id=to,device_id_type=MESH)
        c.start(); pend.append(c)
        return c
    other=1-core
    c=send(g.at[pl.ds(other*HALF,HALF)],rc,at(x,y,z,other))
    c.wait_recv()
    acc[...]=g[pl.ds(core*HALF,HALF)]+rc[...]
    cs=[send(acc.at[pl.ds(((x+d)%XS)*CA,CA)],rx.at[d],at((x+d)%XS,y,z,core)) for d in far_first(XS)]
    for c in cs: c.wait_recv()
    s=acc[pl.ds(x*CA,CA)]
    for d in range(1,XS): s=s+rx[d]
    sx[0:CA]=s
    sx[CA:]=jnp.zeros((YS*CB-CA,8,128),jnp.float32)
    cs=[send(sx.at[pl.ds(((y+d)%YS)*CB,CB)],ry.at[d],at(x,(y+d)%YS,z,core)) for d in far_first(YS)]
    for c in cs: c.wait_recv()
    s=sx[pl.ds(y*CB,CB)]
    for d in range(1,YS): s=s+ry[d]
    sy[...]=s
    cs=[send(sy,rz.at[d],at(x,y,(z+d)%ZS,core)) for d in far_first(ZS)]
    for c in cs: c.wait_recv()
    for d in range(1,ZS): s=s+rz[d]
    gy[pl.ds(y*CB,CB)]=s
    cs=[send(gy.at[pl.ds(y*CB,CB)],gy.at[pl.ds(y*CB,CB)],at(x,(y+d)%YS,z,core)) for d in far_first(YS)]
    for c in cs: c.wait_recv()
    mine=core*HALF+x*CA
    full[pl.ds(mine,CA)]=gy[0:CA]
    cs={d: send(gy.at[pl.ds(0,CA)],full.at[pl.ds(mine,CA)],at((x+d)%XS,y,z,core)) for d in far_first(XS)}
    f0=send(gy.at[pl.ds(0,CA)],full.at[pl.ds(mine,CA)],at(x,y,z,other))
    fs=[f0]
    for d in (1,3,2):
        cs[d].wait_recv()
        src=core*HALF+((x-d+XS)%XS)*CA
        fs.append(send(full.at[pl.ds(src,CA)],full.at[pl.ds(src,CA)],at(x,y,z,other)))
    for c in fs: c.wait_recv()
    for c in pend: c.wait_send()

def barrier(ps):
    sem=pltpu.get_barrier_semaphore()
    for p in ps: pl.semaphore_signal(sem,inc=1,device_id=p,device_id_type=MESH)
    pl.semaphore_wait(sem,len(ps))


DEG = 4
BAND_LOW = 4.0
BAND_HIGH = 34.0
ANCHOR = 0.0
WIDE, NARROW = XS * YS * 2, ZS
PART = 2
COLS = 512 // PART


def coefficients():
    center = (BAND_LOW + BAND_HIGH) / 2.0
    half = (BAND_HIGH - BAND_LOW) / 2.0
    sigma = half / (ANCHOR - center)
    tau = 2.0 / sigma
    out = [(sigma / half, 0.0)]
    for _ in range(DEG - 1):
        fresh = 1.0 / (tau - sigma)
        out.append((2.0 * fresh / half, sigma * fresh))
        sigma = fresh
    return center, out


def filter_scratch():
    f = jnp.float32
    return [
        pltpu.VMEM((512, 512), jnp.bfloat16),
        pltpu.VMEM((DEG, PART, 8, 8, 8, COLS), f),
        pltpu.VMEM((DEG, PART, 8, 8, 8, COLS), f),
        pltpu.VMEM((DEG, PART, 2, 8, 8, COLS), f),
        pltpu.VMEM((DEG, PART, 2, 8, 8, COLS), f),
        pltpu.VMEM((DEG, PART, 2, 2, 8, COLS), f),
        pltpu.SemaphoreType.DMA((DEG + 1, PART, 8)),
        pltpu.SemaphoreType.DMA((DEG + 1, PART, 8)),
    ]


def filter_steps(loads, matrix, order, field, mat, ys, zs, fw, fn, ce, ssem, rsem):
    w = lax.axis_index("wide")
    n = lax.axis_index("narrow")
    wn, wp = (w + 1) % WIDE, (w + WIDE - 1) % WIDE
    nn, np_ = (n + 1) % NARROW, (n + NARROW - 1) % NARROW
    center, weights = coefficients()
    pend = []

    def send(src, dst, r, h, k, to):
        c = pltpu.make_async_remote_copy(
            src_ref=src,
            dst_ref=dst,
            send_sem=ssem.at[r, h, k],
            recv_sem=rsem.at[r, h, k],
            device_id={"wide": to[0], "narrow": to[1]},
            device_id_type=MESH,
        )
        c.start()
        pend.append(c)
        return c

    copies = {}
    for h in range(PART):
        loads[1 + h].wait()
        for i in range(7):
            for j in range(7):
                ys[0, h, i, j, 7:8] = ys[0, h, i, j, 0:1]
        y = ys.at[0, h]
        copies[0, h] = [
            send(y.at[0, 0], y.at[7, 7], 0, h, 2, (wp, np_)),
            send(y.at[0:7, 0], y.at[0:7, 7], 0, h, 1, (w, np_)),
            send(y.at[0, 0:7], y.at[7, 0:7], 0, h, 0, (wp, n)),
        ]
    loads[0].wait()
    loads[1 + PART].wait()
    place_of = jnp.where(
        lax.broadcasted_iota(jnp.int32, (512, 512), 0) == jnp.broadcast_to(order[...], (512, 512)), 1.0, 0.0
    ).astype(jnp.bfloat16)
    rows_placed = jnp.dot(place_of, matrix[...], preferred_element_type=jnp.float32).astype(jnp.bfloat16)
    mat[...] = lax.dot_general(
        rows_placed, place_of, (((1,), (1,)), ((), ())), preferred_element_type=jnp.float32
    ).astype(jnp.bfloat16)

    sub = lax.broadcasted_iota(jnp.int32, (8, 8, COLS), 1)

    def updated(image, r, h, i, j):
        out = (image - center * ys[r, h, i, j]) * weights[r][0]
        if r > 0:
            out = out - weights[r][1] * ys[r - 1, h, i, j]
        return out

    def store(r, h, i, j, value):
        if r < DEG - 1:
            ys[r + 1, h, i, j] = value
        elif not isinstance(i, int) or i < 7:
            field[h, i, j] = value

    def interior(r, h):
        inner = slice(1, 7)
        for i in range(1, 7):
            value = updated(zs[r, h, i, inner], r, h, i, inner)
            if r == DEG - 1:
                value = jnp.where(sub[1:7] < 7, value, 0.0)
            store(r, h, i, inner, value)

    def border(r, h):
        last = r == DEG - 1
        keep = (lambda v: jnp.where(sub[0, :, :] < 7, v, 0.0)) if last else (lambda v: v)
        for i in range(7 if last else 8):
            edge = i in (0, 7)
            for j in range(8) if edge else (0, 7):
                if last and j == 7:
                    field[h, i, 7] = jnp.zeros((8, COLS), jnp.float32)
                    continue
                image = zs[r, h, i, j]
                a, b = (0 if i == 0 else 1), (0 if j == 0 else 1)
                if edge:
                    image = image + fw[r, h, a, j]
                if j in (0, 7):
                    image = image + fn[r, h, b, i]
                    if edge:
                        image = image + ce[r, h, a, b]
                store(r, h, i, j, keep(updated(image, r, h, i, j)))

    for r in range(DEG):
        for h in range(PART):
            for c in copies[r, h]:
                c.wait_recv()
            if r > 0:
                border(r - 1, h)
            rounded = ys[r, h].reshape(512, COLS).astype(jnp.bfloat16)
            product = jnp.dot(mat[...], rounded, preferred_element_type=jnp.float32).reshape(8, 8, 8, COLS)
            for i in range(8):
                v = product[i]
                joined = jnp.where(
                    sub == 0, pltpu.roll(v, 1, axis=1), jnp.where(sub == 7, pltpu.roll(v, 7, axis=1), 0.0)
                )
                zs[r, h, i] = v + joined
            z, gw, gn, gc = zs.at[r, h], fw.at[r, h], fn.at[r, h], ce.at[r, h]
            both = r < DEG - 1
            cs = [send(z.at[7, 7], gc.at[0, 0], r + 1, h, 2, (wn, nn))]
            if both:
                cs += [
                    send(z.at[0, 0], gc.at[1, 1], r + 1, h, 7, (wp, np_)),
                    send(z.at[7, 0], gc.at[0, 1], r + 1, h, 5, (wn, np_)),
                    send(z.at[0, 7], gc.at[1, 0], r + 1, h, 6, (wp, nn)),
                ]
            cs.append(send(z.at[:, 7], gn.at[0], r + 1, h, 1, (w, nn)))
            if both:
                cs.append(send(z.at[:, 0], gn.at[1], r + 1, h, 4, (w, np_)))
            cs.append(send(z.at[7], gw.at[0], r + 1, h, 0, (wn, n)))
            if both:
                cs.append(send(z.at[0], gw.at[1], r + 1, h, 3, (wp, n)))
            copies[r + 1, h] = cs
            interior(r, h)
    for h in range(PART):
        for c in copies[DEG, h]:
            c.wait_recv()
        border(DEG - 1, h)
    return pend


def neighbours(w, n):
    return [
        {"wide": (w + a) % WIDE, "narrow": (n + b) % NARROW}
        for a in (WIDE - 1, 0, 1)
        for b in (NARROW - 1, 0, 1)
        if (a, b) != (0, 0)
    ]


def gram_tiles(field, tiles):
    def dot_tn(a, b):
        return lax.dot_general(
            a, b, (((0,), (0,)), ((), ())), precision=lax.Precision.HIGHEST, preferred_element_type=jnp.float32
        )

    cols = [field[h].reshape(448, COLS) for h in range(PART)]
    per = COLS // 128
    for a in range(PART):
        for b in range(a + 1):
            block = dot_tn(cols[a], cols[b])
            for i in range(per):
                for j in range(per):
                    p, q = a * per + i, b * per + j
                    if q <= p:
                        t = 16 * (p * (p + 1) // 2 + q)
                        tiles[t : t + 16] = block[128 * i : 128 * i + 128, 128 * j : 128 * j + 128].reshape(16, 8, 128)


def filter_kernel(orbitals, matrix, order, field, full, tiles, held, numbers, lsem, *scratch):
    ys = scratch[1]
    loads = [pltpu.make_async_copy(matrix, held, lsem.at[0])] + [
        pltpu.make_async_copy(
            orbitals.at[:, :, :, COLS * h : COLS * h + COLS], ys.at[0, h, 0:7, 0:7, 0:7], lsem.at[1 + h]
        )
        for h in range(PART)
    ]
    loads.append(pltpu.make_async_copy(order, numbers, lsem.at[1 + PART]))
    for c in loads[1:] + loads[:1]:
        c.start()
    barrier(neighbours(lax.axis_index("wide"), lax.axis_index("narrow")) + peers(*place()))
    pend = filter_steps(loads, held, numbers, field, *scratch[:8])
    gram_tiles(field, tiles)
    all_reduce(tiles, full, *scratch[8:])
    for c in pend:
        c.wait_send()


def filter_call(orbitals, matrix, order):
    return pl.pallas_call(
        filter_kernel,
        out_shape=(
            jax.ShapeDtypeStruct((PART, 7, 8, 8, COLS), jnp.float32),
            jax.ShapeDtypeStruct((TILES, 8, 128), jnp.float32),
        ),
        in_specs=[pl.BlockSpec(memory_space=pltpu.HBM)] * 3,
        out_specs=[pl.BlockSpec(memory_space=pltpu.VMEM)] * 2,
        scratch_shapes=[
            pltpu.VMEM((TILES, 8, 128), jnp.float32),
            pltpu.VMEM((512, 512), jnp.bfloat16),
            pltpu.VMEM((1, 512), jnp.int32),
            pltpu.SemaphoreType.DMA((2 + PART,)),
        ] + filter_scratch() + ar_scratch(),
        compiler_params=pltpu.CompilerParams(collective_id=0, has_side_effects=True, vmem_limit_bytes=48 << 20),
    )(*(pltpu.with_memory_space_constraint(a, pltpu.HBM) for a in (orbitals, matrix, order)))


def halves(a):
    high = a.astype(jnp.bfloat16)
    return high, (a - high.astype(jnp.float32)).astype(jnp.bfloat16)


def product(a, b, dims):
    (ah, al), (bh, bl) = halves(a), halves(b)

    def one(p, q):
        return lax.dot_general(p, q, (dims, ((), ())), preferred_element_type=jnp.float32)

    return one(ah, bh) + (one(ah, bl) + one(al, bh))


def dot_nn(a, b):
    return product(a, b, ((1,), (0,)))


def dot_nt(a, b):
    return product(a, b, ((1,), (1,)))


def reciprocal(d):
    r = pl.reciprocal(d, approx=True)
    return r * (2.0 - d * r)


def thirds(a):
    high = a.astype(jnp.bfloat16).astype(jnp.float32)
    rest = a - high
    middle = rest.astype(jnp.bfloat16).astype(jnp.float32)
    return high, middle, rest - middle


def outer(r, s):
    (rh, rm, rl), (sh, sm, sl) = thirds(r), thirds(s)
    left = jnp.concatenate([rh, rh, rm, rm, rh, rl], axis=0).astype(jnp.bfloat16)
    right = jnp.concatenate([sh, sm, sh, sm, sl, sh], axis=0).astype(jnp.bfloat16)
    return lax.dot_general(left, right, (((0,), (0,)), ((), ())), preferred_element_type=jnp.float32)


def inverse_factor(block):
    rows = [block[8 * i : 8 * i + 8, :] for i in range(16)]
    lane = lax.broadcasted_iota(jnp.int32, (8, 128), 1)
    sub = lax.broadcasted_iota(jnp.int32, (8, 128), 0)
    for b in range(16):
        first = 8 * b
        panel = [jnp.broadcast_to(rows[b][i : i + 1, :], (8, 128)) for i in range(8)]
        e = {}
        for i in range(8):
            for j in range(i, 8):
                e[i, j] = jnp.broadcast_to(panel[i][:, first + j : first + j + 1], (8, 128))
        inside = (lane >= first) & (lane < first + 8)
        p = [jnp.where(inside, jnp.where(lane == first + i, 1.0, 0.0), panel[i]) for i in range(8)]
        if b < 15:
            below = rows[b + 1]
            c = [jnp.broadcast_to(below[:, first + k : first + k + 1], (8, 128)) for k in range(8)]
        inv = [None] * 8
        m = {}
        for k in range(0, 8, 2):
            u, v, t = e[k, k], e[k, k + 1], e[k + 1, k + 1]
            det = u * t - v * v
            over = reciprocal(det)
            iu, iv, it = t * over, v * over, u * over
            inv[k] = reciprocal(u)
            inv[k + 1] = it
            m[k + 1, k] = v * inv[k]
            e[k + 1, k + 1] = det * inv[k]
            for i in range(k + 2, 8):
                f, g = e[k, i], e[k + 1, i]
                one, two = f * iu - g * iv, g * it - f * iv
                for j in range(i, 8):
                    e[i, j] = e[i, j] - (one * e[k, j] + two * e[k + 1, j])
                m[i, k], m[i, k + 1] = f * inv[k], two
            p[k + 1] = p[k + 1] - m[k + 1, k] * p[k]
            for i in range(k + 2, 8):
                p[i] = p[i] - (m[i, k] * p[k] + m[i, k + 1] * p[k + 1])
        own, pivot = p[0], e[0, 0]
        for k in range(1, 8):
            own = jnp.where(sub == k, p[k], own)
            pivot = jnp.where(sub == k, e[k, k], pivot)
        if b < 15:
            s = [p[k] * inv[k] for k in range(8)]
            for l in range(6, -1, -1):
                for k in range(7, l, -1):
                    s[l] = s[l] - m[k, l] * s[k]
            terms = [c[k] * s[k] for k in range(8)]
            while len(terms) > 1:
                terms = [terms[i] + terms[i + 1] for i in range(0, len(terms), 2)]
            fresh = jnp.where(inside, 0.0, below) - terms[0]
            if b < 14:
                change = outer(own, own * reciprocal(pivot))
                for i in range(b + 2, 16):
                    rows[i] = jnp.where(inside, 0.0, rows[i]) - change[8 * i : 8 * i + 8]
            rows[b + 1] = fresh
        y = lax.rsqrt(pivot)
        y = y * (1.5 - 0.5 * pivot * y * y)
        rows[b] = jnp.where(lane <= sub + first, own, 0.0) * y
    return jnp.concatenate(rows, axis=0)


def finish_kernel(node_total, packed, field, out, w, x, f):
    on_diagonal = lax.broadcasted_iota(jnp.int32, (128, 128), 0) == lax.broadcasted_iota(jnp.int32, (128, 128), 1)

    def block(i, j):
        at_tile = 16 * (i * (i + 1) // 2 + j)
        return packed[at_tile : at_tile + 16].reshape(128, 128) * (1.0 / node_total)

    scale_row, scale_column = [], []
    for i in range(4):
        diagonal = jnp.where(on_diagonal, block(i, i), 0.0)
        s = jnp.broadcast_to(lax.rsqrt(jnp.sum(diagonal, axis=0, keepdims=True)), (128, 128))
        scale_row.append(s)
        scale_column.append(jnp.broadcast_to(jnp.sum(jnp.where(on_diagonal, s, 0.0), axis=1, keepdims=True), (128, 128)))
    for i in range(4):
        for j in range(i + 1):
            w[128 * i : 128 * i + 128, 128 * j : 128 * j + 128] = block(i, j) * scale_column[i] * scale_row[j]
    for j in range(4):
        h, q = divmod(128 * j, COLS)
        cols = field[h].reshape(448, COLS)[:, q : q + 128]
        f[:, 128 * j : 128 * j + 128] = cols * scale_row[j][0:1, :]
    lower = {}
    for j in range(4):
        here = slice(128 * j, 128 * j + 128)
        inverse = inverse_factor(w[here, here])
        if j < 3:
            column = dot_nt(w[128 * (j + 1) :, here], inverse)
            lower[j] = column
            for i in range(j + 1, 4):
                band = column[128 * (i - j - 1) : 128 * (i - j)]
                w[128 * i : 128 * i + 128, 128 * (j + 1) : 128 * (i + 1)] = w[
                    128 * i : 128 * i + 128, 128 * (j + 1) : 128 * (i + 1)
                ] - dot_nt(band, column[: 128 * (i - j)])
        x[here, here] = inverse
        if j > 0:
            left = jnp.concatenate([lower[k][128 * (j - k - 1) : 128 * (j - k)] for k in range(j)], axis=1)
            x[here, : 128 * j] = -dot_nn(inverse, dot_nn(left, x[: 128 * j, : 128 * j]))
        rotated = dot_nt(f[:, : 128 * (j + 1)], x[here, : 128 * (j + 1)])
        for a in range(7):
            for b in range(7):
                r = 64 * a + 8 * b
                out[a, b, :, here] = rotated[r : r + 7, :]
        if j < 3:
            x[here, 128 * (j + 1) :] = jnp.zeros((128, 512 - 128 * (j + 1)), jnp.float32)


def finish_call(packed, field, node_total):
    return pl.pallas_call(
        functools.partial(finish_kernel, node_total),
        out_shape=jax.ShapeDtypeStruct((7, 7, 7, 512), jnp.float32),
        in_specs=[pl.BlockSpec(memory_space=pltpu.VMEM)] * 2,
        out_specs=pl.BlockSpec(memory_space=pltpu.VMEM),
        scratch_shapes=[
            pltpu.VMEM((512, 512), jnp.float32),
            pltpu.VMEM((512, 512), jnp.float32),
            pltpu.VMEM((448, 512), jnp.float32),
        ],
        compiler_params=pltpu.CompilerParams(vmem_limit_bytes=40 << 20),
    )(packed, field)


def on_device(orbitals, cell_matrix, cell_order):
    node_total = 343.0 * WIDE * NARROW
    field, total = filter_call(orbitals, cell_matrix.reshape(512, 512), cell_order.reshape(1, 512))
    return finish_call(total, field, node_total)


def solution(mesh):
    return jax.shard_map(
        on_device,
        mesh=mesh,
        in_specs=(
            P("wide", "narrow", None, None),
            P("wide", "narrow", None, None, None),
            P("wide", "narrow", None, None),
        ),
        out_specs=P("wide", "narrow", None, None),
        check_vma=False,
    )
```

```python
import functools

import jax
import jax.numpy as jnp
from jax import lax
from jax.experimental import pallas as pl
from jax.experimental.pallas import tpu as pltpu
from jax.sharding import PartitionSpec as P

MESH=pl.DeviceIdType.MESH
XS,YS,ZS=4,8,8
TILES=160
HALF=TILES//2
CA=HALF//XS
CB=3


def far_first(count):
    return sorted(range(1,count),key=lambda d:-min(d,count-d))

def place():
    w=lax.axis_index("wide"); z=lax.axis_index("narrow")
    x=w//16; y=(w//2)%8; core=w%2
    return x,y,z,core

def at(x,y,z,core):
    return {"wide": x*16+y*2+core, "narrow": z}

def peers(x,y,z,core):
    out=[at(x,y,z,1-core)]
    for d in range(1,XS): out.append(at((x+d)%XS,y,z,core))
    for d in range(1,YS): out.append(at(x,(y+d)%YS,z,core))
    for d in range(1,ZS): out.append(at(x,y,(z+d)%ZS,core))
    return out

def ar_scratch():
    f=jnp.float32
    return [pltpu.VMEM((HALF,8,128),f),
            pltpu.VMEM((HALF,8,128),f),
            pltpu.VMEM((XS,CA,8,128),f),
            pltpu.VMEM((YS*CB,8,128),f),
            pltpu.VMEM((YS,CB,8,128),f),
            pltpu.VMEM((CB,8,128),f),
            pltpu.VMEM((ZS,CB,8,128),f),
            pltpu.VMEM((YS*CB,8,128),f),
            pltpu.SemaphoreType.DMA((40,)),
            pltpu.SemaphoreType.DMA((40,))]

def all_reduce(g, full, rc, acc, rx, sx, ry, sy, rz, gy, ssem, rsem):
    x,y,z,core=place()
    pend=[]
    cnt=[0]
    def send(src,dst,to):
        k=cnt[0]; cnt[0]+=1
        c=pltpu.make_async_remote_copy(src_ref=src,dst_ref=dst,send_sem=ssem.at[k],recv_sem=rsem.at[k],device_id=to,device_id_type=MESH)
        c.start(); pend.append(c)
        return c
    other=1-core
    c=send(g.at[pl.ds(other*HALF,HALF)],rc,at(x,y,z,other))
    c.wait_recv()
    acc[...]=g[pl.ds(core*HALF,HALF)]+rc[...]
    cs=[send(acc.at[pl.ds(((x+d)%XS)*CA,CA)],rx.at[d],at((x+d)%XS,y,z,core)) for d in far_first(XS)]
    for c in cs: c.wait_recv()
    s=acc[pl.ds(x*CA,CA)]
    for d in range(1,XS): s=s+rx[d]
    sx[0:CA]=s
    sx[CA:]=jnp.zeros((YS*CB-CA,8,128),jnp.float32)
    cs=[send(sx.at[pl.ds(((y+d)%YS)*CB,CB)],ry.at[d],at(x,(y+d)%YS,z,core)) for d in far_first(YS)]
    for c in cs: c.wait_recv()
    s=sx[pl.ds(y*CB,CB)]
    for d in range(1,YS): s=s+ry[d]
    sy[...]=s
    cs=[send(sy,rz.at[d],at(x,y,(z+d)%ZS,core)) for d in far_first(ZS)]
    for c in cs: c.wait_recv()
    for d in range(1,ZS): s=s+rz[d]
    gy[pl.ds(y*CB,CB)]=s
    cs=[send(gy.at[pl.ds(y*CB,CB)],gy.at[pl.ds(y*CB,CB)],at(x,(y+d)%YS,z,core)) for d in far_first(YS)]
    for c in cs: c.wait_recv()
    mine=core*HALF+x*CA
    full[pl.ds(mine,CA)]=gy[0:CA]
    cs={d: send(gy.at[pl.ds(0,CA)],full.at[pl.ds(mine,CA)],at((x+d)%XS,y,z,core)) for d in far_first(XS)}
    f0=send(gy.at[pl.ds(0,CA)],full.at[pl.ds(mine,CA)],at(x,y,z,other))
    fs=[f0]
    for d in (1,3,2):
        cs[d].wait_recv()
        src=core*HALF+((x-d+XS)%XS)*CA
        fs.append(send(full.at[pl.ds(src,CA)],full.at[pl.ds(src,CA)],at(x,y,z,other)))
    for c in fs: c.wait_recv()
    for c in pend: c.wait_send()

def barrier(ps):
    sem=pltpu.get_barrier_semaphore()
    for p in ps: pl.semaphore_signal(sem,inc=1,device_id=p,device_id_type=MESH)
    pl.semaphore_wait(sem,len(ps))


DEG = 4
BAND_LOW = 4.0
BAND_HIGH = 34.0
ANCHOR = 0.0
WIDE, NARROW = XS * YS * 2, ZS
PART = 2
COLS = 512 // PART


def coefficients():
    center = (BAND_LOW + BAND_HIGH) / 2.0
    half = (BAND_HIGH - BAND_LOW) / 2.0
    sigma = half / (ANCHOR - center)
    tau = 2.0 / sigma
    out = [(sigma / half, 0.0)]
    for _ in range(DEG - 1):
        fresh = 1.0 / (tau - sigma)
        out.append((2.0 * fresh / half, sigma * fresh))
        sigma = fresh
    return center, out


def filter_scratch():
    f = jnp.float32
    return [
        pltpu.VMEM((512, 512), jnp.bfloat16),
        pltpu.VMEM((DEG, PART, 8, 8, 8, COLS), f),
        pltpu.VMEM((DEG, PART, 8, 8, 8, COLS), f),
        pltpu.VMEM((DEG, PART, 2, 8, 8, COLS), f),
        pltpu.VMEM((DEG, PART, 2, 8, 8, COLS), f),
        pltpu.VMEM((DEG, PART, 2, 2, 8, COLS), f),
        pltpu.SemaphoreType.DMA((DEG + 1, PART, 8)),
        pltpu.SemaphoreType.DMA((DEG + 1, PART, 8)),
    ]


def filter_steps(loads, matrix, order, field, mat, ys, zs, fw, fn, ce, ssem, rsem):
    w = lax.axis_index("wide")
    n = lax.axis_index("narrow")
    wn, wp = (w + 1) % WIDE, (w + WIDE - 1) % WIDE
    nn, np_ = (n + 1) % NARROW, (n + NARROW - 1) % NARROW
    center, weights = coefficients()
    pend = []

    def send(src, dst, r, h, k, to):
        c = pltpu.make_async_remote_copy(
            src_ref=src,
            dst_ref=dst,
            send_sem=ssem.at[r, h, k],
            recv_sem=rsem.at[r, h, k],
            device_id={"wide": to[0], "narrow": to[1]},
            device_id_type=MESH,
        )
        c.start()
        pend.append(c)
        return c

    copies = {}
    for h in range(PART):
        loads[1 + h].wait()
        for i in range(7):
            for j in range(7):
                ys[0, h, i, j, 7:8] = ys[0, h, i, j, 0:1]
        y = ys.at[0, h]
        copies[0, h] = [
            send(y.at[0, 0], y.at[7, 7], 0, h, 2, (wp, np_)),
            send(y.at[0:7, 0], y.at[0:7, 7], 0, h, 1, (w, np_)),
            send(y.at[0, 0:7], y.at[7, 0:7], 0, h, 0, (wp, n)),
        ]
    loads[0].wait()
    loads[1 + PART].wait()
    place_of = jnp.where(
        lax.broadcasted_iota(jnp.int32, (512, 512), 0) == jnp.broadcast_to(order[...], (512, 512)), 1.0, 0.0
    ).astype(jnp.bfloat16)
    rows_placed = jnp.dot(place_of, matrix[...], preferred_element_type=jnp.float32).astype(jnp.bfloat16)
    mat[...] = lax.dot_general(
        rows_placed, place_of, (((1,), (1,)), ((), ())), preferred_element_type=jnp.float32
    ).astype(jnp.bfloat16)

    sub = lax.broadcasted_iota(jnp.int32, (8, 8, COLS), 1)

    def updated(image, r, h, i, j):
        out = (image - center * ys[r, h, i, j]) * weights[r][0]
        if r > 0:
            out = out - weights[r][1] * ys[r - 1, h, i, j]
        return out

    def store(r, h, i, j, value):
        if r < DEG - 1:
            ys[r + 1, h, i, j] = value
        elif not isinstance(i, int) or i < 7:
            field[h, i, j] = value

    def interior(r, h):
        inner = slice(1, 7)
        for i in range(1, 7):
            value = updated(zs[r, h, i, inner], r, h, i, inner)
            if r == DEG - 1:
                value = jnp.where(sub[1:7] < 7, value, 0.0)
            store(r, h, i, inner, value)

    def border(r, h):
        last = r == DEG - 1
        keep = (lambda v: jnp.where(sub[0, :, :] < 7, v, 0.0)) if last else (lambda v: v)
        for i in range(7 if last else 8):
            edge = i in (0, 7)
            for j in range(8) if edge else (0, 7):
                if last and j == 7:
                    field[h, i, 7] = jnp.zeros((8, COLS), jnp.float32)
                    continue
                image = zs[r, h, i, j]
                a, b = (0 if i == 0 else 1), (0 if j == 0 else 1)
                if edge:
                    image = image + fw[r, h, a, j]
                if j in (0, 7):
                    image = image + fn[r, h, b, i]
                    if edge:
                        image = image + ce[r, h, a, b]
                store(r, h, i, j, keep(updated(image, r, h, i, j)))

    for r in range(DEG):
        for h in range(PART):
            for c in copies[r, h]:
                c.wait_recv()
            if r > 0:
                border(r - 1, h)
            rounded = ys[r, h].reshape(512, COLS).astype(jnp.bfloat16)
            product = jnp.dot(mat[...], rounded, preferred_element_type=jnp.float32).reshape(8, 8, 8, COLS)
            for i in range(8):
                v = product[i]
                joined = jnp.where(
                    sub == 0, pltpu.roll(v, 1, axis=1), jnp.where(sub == 7, pltpu.roll(v, 7, axis=1), 0.0)
                )
                zs[r, h, i] = v + joined
            z, gw, gn, gc = zs.at[r, h], fw.at[r, h], fn.at[r, h], ce.at[r, h]
            both = r < DEG - 1
            cs = [send(z.at[7, 7], gc.at[0, 0], r + 1, h, 2, (wn, nn))]
            if both:
                cs += [
                    send(z.at[0, 0], gc.at[1, 1], r + 1, h, 7, (wp, np_)),
                    send(z.at[7, 0], gc.at[0, 1], r + 1, h, 5, (wn, np_)),
                    send(z.at[0, 7], gc.at[1, 0], r + 1, h, 6, (wp, nn)),
                ]
            cs.append(send(z.at[:, 7], gn.at[0], r + 1, h, 1, (w, nn)))
            if both:
                cs.append(send(z.at[:, 0], gn.at[1], r + 1, h, 4, (w, np_)))
            cs.append(send(z.at[7], gw.at[0], r + 1, h, 0, (wn, n)))
            if both:
                cs.append(send(z.at[0], gw.at[1], r + 1, h, 3, (wp, n)))
            copies[r + 1, h] = cs
            interior(r, h)
    for h in range(PART):
        for c in copies[DEG, h]:
            c.wait_recv()
        border(DEG - 1, h)
    return pend


def neighbours(w, n):
    return [
        {"wide": (w + a) % WIDE, "narrow": (n + b) % NARROW}
        for a in (WIDE - 1, 0, 1)
        for b in (NARROW - 1, 0, 1)
        if (a, b) != (0, 0)
    ]


def halves(a):
    high = a.astype(jnp.bfloat16)
    return high, (a - high.astype(jnp.float32)).astype(jnp.bfloat16)


def dot_tn(a, b):
    return lax.dot_general(a, b, (((0,), (0,)), ((), ())), preferred_element_type=jnp.float32)


def gram_tiles(field, tiles):
    cols = [halves(field[h].reshape(448, COLS)) for h in range(PART)]
    per = COLS // 128
    for a in range(PART):
        for b in range(a + 1):
            (ah, al), (bh, bl) = cols[a], cols[b]
            block = dot_tn(ah, bh) + (dot_tn(ah, bl) + dot_tn(al, bh))
            for i in range(per):
                for j in range(per):
                    p, q = a * per + i, b * per + j
                    if q <= p:
                        t = 16 * (p * (p + 1) // 2 + q)
                        tiles[t : t + 16] = block[128 * i : 128 * i + 128, 128 * j : 128 * j + 128].reshape(16, 8, 128)


def filter_kernel(orbitals, matrix, order, field, full, tiles, held, numbers, lsem, *scratch):
    ys = scratch[1]
    loads = [pltpu.make_async_copy(matrix, held, lsem.at[0])] + [
        pltpu.make_async_copy(
            orbitals.at[:, :, :, COLS * h : COLS * h + COLS], ys.at[0, h, 0:7, 0:7, 0:7], lsem.at[1 + h]
        )
        for h in range(PART)
    ]
    loads.append(pltpu.make_async_copy(order, numbers, lsem.at[1 + PART]))
    for c in loads[1:] + loads[:1]:
        c.start()
    barrier(neighbours(lax.axis_index("wide"), lax.axis_index("narrow")) + peers(*place()))
    pend = filter_steps(loads, held, numbers, field, *scratch[:8])
    gram_tiles(field, tiles)
    all_reduce(tiles, full, *scratch[8:])
    for c in pend:
        c.wait_send()


def filter_call(orbitals, matrix, order):
    return pl.pallas_call(
        filter_kernel,
        out_shape=(
            jax.ShapeDtypeStruct((PART, 7, 8, 8, COLS), jnp.float32),
            jax.ShapeDtypeStruct((TILES, 8, 128), jnp.float32),
        ),
        in_specs=[pl.BlockSpec(memory_space=pltpu.HBM)] * 3,
        out_specs=[pl.BlockSpec(memory_space=pltpu.VMEM)] * 2,
        scratch_shapes=[
            pltpu.VMEM((TILES, 8, 128), jnp.float32),
            pltpu.VMEM((512, 512), jnp.bfloat16),
            pltpu.VMEM((1, 512), jnp.int32),
            pltpu.SemaphoreType.DMA((2 + PART,)),
        ] + filter_scratch() + ar_scratch(),
        compiler_params=pltpu.CompilerParams(collective_id=0, has_side_effects=True, vmem_limit_bytes=48 << 20),
    )(*(pltpu.with_memory_space_constraint(a, pltpu.HBM) for a in (orbitals, matrix, order)))


def product(a, b, dims):
    (ah, al), (bh, bl) = halves(a), halves(b)

    def one(p, q):
        return lax.dot_general(p, q, (dims, ((), ())), preferred_element_type=jnp.float32)

    return one(ah, bh) + (one(ah, bl) + one(al, bh))


def dot_nt(a, b):
    return product(a, b, ((1,), (1,)))


def reciprocal(d):
    r = pl.reciprocal(d, approx=True)
    return r * (2.0 - d * r)


def thirds(a):
    high = a.astype(jnp.bfloat16).astype(jnp.float32)
    rest = a - high
    middle = rest.astype(jnp.bfloat16).astype(jnp.float32)
    return high, middle, rest - middle


def outer(r, s):
    (rh, rm, rl), (sh, sm, sl) = thirds(r), thirds(s)
    left = jnp.concatenate([rh, rh, rm, rm, rh, rl], axis=0).astype(jnp.bfloat16)
    right = jnp.concatenate([sh, sm, sh, sm, sl, sh], axis=0).astype(jnp.bfloat16)
    return lax.dot_general(left, right, (((0,), (0,)), ((), ())), preferred_element_type=jnp.float32)


def inverse_factor(block):
    rows = [block[8 * i : 8 * i + 8, :] for i in range(16)]
    lane = lax.broadcasted_iota(jnp.int32, (8, 128), 1)
    sub = lax.broadcasted_iota(jnp.int32, (8, 128), 0)
    for b in range(16):
        first = 8 * b
        panel = [jnp.broadcast_to(rows[b][i : i + 1, :], (8, 128)) for i in range(8)]
        e = {}
        for i in range(8):
            for j in range(i, 8):
                e[i, j] = jnp.broadcast_to(panel[i][:, first + j : first + j + 1], (8, 128))
        inside = (lane >= first) & (lane < first + 8)
        p = [jnp.where(inside, jnp.where(lane == first + i, 1.0, 0.0), panel[i]) for i in range(8)]
        if b < 15:
            below = rows[b + 1]
            c = [jnp.broadcast_to(below[:, first + k : first + k + 1], (8, 128)) for k in range(8)]
        inv = [None] * 8
        m = {}
        for k in range(0, 8, 2):
            u, v, t = e[k, k], e[k, k + 1], e[k + 1, k + 1]
            det = u * t - v * v
            over = reciprocal(det)
            iu, iv, it = t * over, v * over, u * over
            inv[k] = reciprocal(u)
            inv[k + 1] = it
            m[k + 1, k] = v * inv[k]
            e[k + 1, k + 1] = det * inv[k]
            for i in range(k + 2, 8):
                f, g = e[k, i], e[k + 1, i]
                one, two = f * iu - g * iv, g * it - f * iv
                for j in range(i, 8):
                    e[i, j] = e[i, j] - (one * e[k, j] + two * e[k + 1, j])
                m[i, k], m[i, k + 1] = f * inv[k], two
            p[k + 1] = p[k + 1] - m[k + 1, k] * p[k]
            for i in range(k + 2, 8):
                p[i] = p[i] - (m[i, k] * p[k] + m[i, k + 1] * p[k + 1])
        own, pivot = p[0], e[0, 0]
        for k in range(1, 8):
            own = jnp.where(sub == k, p[k], own)
            pivot = jnp.where(sub == k, e[k, k], pivot)
        if b < 15:
            s = [p[k] * inv[k] for k in range(8)]
            for l in range(6, -1, -1):
                for k in range(7, l, -1):
                    s[l] = s[l] - m[k, l] * s[k]
            terms = [c[k] * s[k] for k in range(8)]
            while len(terms) > 1:
                terms = [terms[i] + terms[i + 1] for i in range(0, len(terms), 2)]
            fresh = jnp.where(inside, 0.0, below) - terms[0]
            if b < 14:
                change = outer(own, own * reciprocal(pivot))
                for i in range(b + 2, 16):
                    rows[i] = jnp.where(inside, 0.0, rows[i]) - change[8 * i : 8 * i + 8]
            rows[b + 1] = fresh
        y = lax.rsqrt(pivot)
        y = y * (1.5 - 0.5 * pivot * y * y)
        rows[b] = jnp.where(lane <= sub + first, own, 0.0) * y
    return jnp.concatenate(rows, axis=0)


def finish_kernel(node_total, packed, field, out, w, f, held, sems):
    on_diagonal = lax.broadcasted_iota(jnp.int32, (128, 128), 0) == lax.broadcasted_iota(jnp.int32, (128, 128), 1)

    def block(i, j):
        at_tile = 16 * (i * (i + 1) // 2 + j)
        return packed[at_tile : at_tile + 16].reshape(128, 128) * (1.0 / node_total)

    scale_row, scale_column = [], []
    for i in range(4):
        diagonal = jnp.where(on_diagonal, block(i, i), 0.0)
        s = jnp.broadcast_to(lax.rsqrt(jnp.sum(diagonal, axis=0, keepdims=True)), (128, 128))
        scale_row.append(s)
        scale_column.append(jnp.broadcast_to(jnp.sum(jnp.where(on_diagonal, s, 0.0), axis=1, keepdims=True), (128, 128)))
    for i in range(4):
        for j in range(i + 1):
            w[128 * i : 128 * i + 128, 128 * j : 128 * j + 128] = block(i, j) * scale_column[i] * scale_row[j]
    for j in range(4):
        h, q = divmod(128 * j, COLS)
        cols = field[h].reshape(448, COLS)[:, q : q + 128]
        f[:, 128 * j : 128 * j + 128] = cols * scale_row[j][0:1, :]
    stores = []
    for j in range(4):
        here = slice(128 * j, 128 * j + 128)
        inverse = inverse_factor(w[here, here])
        if j < 3:
            column = dot_nt(w[128 * (j + 1) :, here], inverse)
            for i in range(j + 1, 4):
                band = column[128 * (i - j - 1) : 128 * (i - j)]
                w[128 * i : 128 * i + 128, 128 * (j + 1) : 128 * (i + 1)] = w[
                    128 * i : 128 * i + 128, 128 * (j + 1) : 128 * (i + 1)
                ] - dot_nt(band, column[: 128 * (i - j)])
        rotated = dot_nt(f[:, here], inverse)
        held[:, :, :, here] = rotated.reshape(7, 8, 8, 128)
        stores.append(
            pltpu.make_async_copy(held.at[:, 0:7, 0:7, here], out.at[:, :, :, here], sems.at[j])
        )
        stores[j].start()
        if j < 3:
            f[:, 128 * (j + 1) :] = f[:, 128 * (j + 1) :] - dot_nt(rotated, column)
    for c in stores:
        c.wait()


def finish_call(packed, field, node_total):
    return pl.pallas_call(
        functools.partial(finish_kernel, node_total),
        out_shape=jax.ShapeDtypeStruct((7, 7, 7, 512), jnp.float32),
        in_specs=[pl.BlockSpec(memory_space=pltpu.VMEM)] * 2,
        out_specs=pl.BlockSpec(memory_space=pltpu.HBM),
        scratch_shapes=[
            pltpu.VMEM((512, 512), jnp.float32),
            pltpu.VMEM((448, 512), jnp.float32),
            pltpu.VMEM((7, 8, 8, 512), jnp.float32),
            pltpu.SemaphoreType.DMA((4,)),
        ],
        compiler_params=pltpu.CompilerParams(vmem_limit_bytes=40 << 20),
    )(packed, field)


def on_device(orbitals, cell_matrix, cell_order):
    node_total = 343.0 * WIDE * NARROW
    field, total = filter_call(orbitals, cell_matrix.reshape(512, 512), cell_order.reshape(1, 512))
    return finish_call(total, field, node_total)


def solution(mesh):
    return jax.shard_map(
        on_device,
        mesh=mesh,
        in_specs=(
            P("wide", "narrow", None, None),
            P("wide", "narrow", None, None, None),
            P("wide", "narrow", None, None),
        ),
        out_specs=P("wide", "narrow", None, None),
        check_vma=False,
    )
```

```python
import functools

import jax
import jax.numpy as jnp
from jax import lax
from jax.experimental import pallas as pl
from jax.experimental.pallas import tpu as pltpu
from jax.sharding import PartitionSpec as P

MESH=pl.DeviceIdType.MESH
XS,YS,ZS=4,8,8
TILES=160
HALF=TILES//2
CA=HALF//XS
CB=3


def far_first(count):
    return sorted(range(1,count),key=lambda d:-min(d,count-d))

def place():
    w=lax.axis_index("wide"); z=lax.axis_index("narrow")
    x=w//16; y=(w//2)%8; core=w%2
    return x,y,z,core

def at(x,y,z,core):
    return {"wide": x*16+y*2+core, "narrow": z}

def peers(x,y,z,core):
    out=[at(x,y,z,1-core)]
    for d in range(1,XS): out.append(at((x+d)%XS,y,z,core))
    for d in range(1,YS): out.append(at(x,(y+d)%YS,z,core))
    for d in range(1,ZS): out.append(at(x,y,(z+d)%ZS,core))
    return out

def ar_scratch():
    f=jnp.float32
    return [pltpu.VMEM((HALF,8,128),f),
            pltpu.VMEM((HALF,8,128),f),
            pltpu.VMEM((XS,CA,8,128),f),
            pltpu.VMEM((YS*CB,8,128),f),
            pltpu.VMEM((YS,CB,8,128),f),
            pltpu.VMEM((CB,8,128),f),
            pltpu.VMEM((ZS,CB,8,128),f),
            pltpu.VMEM((YS*CB,8,128),f),
            pltpu.SemaphoreType.DMA((40,)),
            pltpu.SemaphoreType.DMA((40,))]

def all_reduce(g, full, rc, acc, rx, sx, ry, sy, rz, gy, ssem, rsem):
    x,y,z,core=place()
    pend=[]
    cnt=[0]
    def send(src,dst,to):
        k=cnt[0]; cnt[0]+=1
        c=pltpu.make_async_remote_copy(src_ref=src,dst_ref=dst,send_sem=ssem.at[k],recv_sem=rsem.at[k],device_id=to,device_id_type=MESH)
        c.start(); pend.append(c)
        return c
    other=1-core
    c=send(g.at[pl.ds(other*HALF,HALF)],rc,at(x,y,z,other))
    c.wait_recv()
    acc[...]=g[pl.ds(core*HALF,HALF)]+rc[...]
    cs=[send(acc.at[pl.ds(((x+d)%XS)*CA,CA)],rx.at[d],at((x+d)%XS,y,z,core)) for d in far_first(XS)]
    for c in cs: c.wait_recv()
    s=acc[pl.ds(x*CA,CA)]
    for d in range(1,XS): s=s+rx[d]
    sx[0:CA]=s
    sx[CA:]=jnp.zeros((YS*CB-CA,8,128),jnp.float32)
    cs=[send(sx.at[pl.ds(((y+d)%YS)*CB,CB)],ry.at[d],at(x,(y+d)%YS,z,core)) for d in far_first(YS)]
    for c in cs: c.wait_recv()
    s=sx[pl.ds(y*CB,CB)]
    for d in range(1,YS): s=s+ry[d]
    sy[...]=s
    cs=[send(sy,rz.at[d],at(x,y,(z+d)%ZS,core)) for d in far_first(ZS)]
    for c in cs: c.wait_recv()
    for d in range(1,ZS): s=s+rz[d]
    gy[pl.ds(y*CB,CB)]=s
    cs=[send(gy.at[pl.ds(y*CB,CB)],gy.at[pl.ds(y*CB,CB)],at(x,(y+d)%YS,z,core)) for d in far_first(YS)]
    for c in cs: c.wait_recv()
    mine=core*HALF+x*CA
    full[pl.ds(mine,CA)]=gy[0:CA]
    cs={d: send(gy.at[pl.ds(0,CA)],full.at[pl.ds(mine,CA)],at((x+d)%XS,y,z,core)) for d in far_first(XS)}
    f0=send(gy.at[pl.ds(0,CA)],full.at[pl.ds(mine,CA)],at(x,y,z,other))
    fs=[f0]
    for d in (1,3,2):
        cs[d].wait_recv()
        src=core*HALF+((x-d+XS)%XS)*CA
        fs.append(send(full.at[pl.ds(src,CA)],full.at[pl.ds(src,CA)],at(x,y,z,other)))
    for c in fs: c.wait_recv()
    for c in pend: c.wait_send()

def barrier(ps):
    sem=pltpu.get_barrier_semaphore()
    for p in ps: pl.semaphore_signal(sem,inc=1,device_id=p,device_id_type=MESH)
    pl.semaphore_wait(sem,len(ps))


DEG = 4
BAND_LOW = 4.0
BAND_HIGH = 34.0
ANCHOR = 0.0
WIDE, NARROW = XS * YS * 2, ZS
PART = 2
COLS = 512 // PART


def coefficients():
    center = (BAND_LOW + BAND_HIGH) / 2.0
    half = (BAND_HIGH - BAND_LOW) / 2.0
    sigma = half / (ANCHOR - center)
    tau = 2.0 / sigma
    out = [(sigma / half, 0.0)]
    for _ in range(DEG - 1):
        fresh = 1.0 / (tau - sigma)
        out.append((2.0 * fresh / half, sigma * fresh))
        sigma = fresh
    return center, out


def filter_scratch():
    f = jnp.float32
    return [
        pltpu.VMEM((512, 512), jnp.bfloat16),
        pltpu.VMEM((DEG, PART, 8, 8, 8, COLS), f),
        pltpu.VMEM((DEG, PART, 8, 8, 8, COLS), f),
        pltpu.VMEM((DEG, PART, 2, 8, 8, COLS), f),
        pltpu.VMEM((DEG, PART, 2, 8, 8, COLS), f),
        pltpu.VMEM((DEG, PART, 2, 2, 8, COLS), f),
        pltpu.SemaphoreType.DMA((DEG + 1, PART, 8)),
        pltpu.SemaphoreType.DMA((DEG + 1, PART, 8)),
    ]


def filter_steps(finished, loads, matrix, order, field, mat, ys, zs, fw, fn, ce, ssem, rsem):
    w = lax.axis_index("wide")
    n = lax.axis_index("narrow")
    wn, wp = (w + 1) % WIDE, (w + WIDE - 1) % WIDE
    nn, np_ = (n + 1) % NARROW, (n + NARROW - 1) % NARROW
    center, weights = coefficients()
    pend = []

    def send(src, dst, r, h, k, to):
        c = pltpu.make_async_remote_copy(
            src_ref=src,
            dst_ref=dst,
            send_sem=ssem.at[r, h, k],
            recv_sem=rsem.at[r, h, k],
            device_id={"wide": to[0], "narrow": to[1]},
            device_id_type=MESH,
        )
        c.start()
        pend.append(c)
        return c

    copies = {}
    for h in range(PART):
        loads[1 + h].wait()
        for i in range(7):
            for j in range(7):
                ys[0, h, i, j, 7:8] = ys[0, h, i, j, 0:1]
        y = ys.at[0, h]
        copies[0, h] = [
            send(y.at[0, 0], y.at[7, 7], 0, h, 2, (wp, np_)),
            send(y.at[0:7, 0], y.at[0:7, 7], 0, h, 1, (w, np_)),
            send(y.at[0, 0:7], y.at[7, 0:7], 0, h, 0, (wp, n)),
        ]
    loads[0].wait()
    loads[1 + PART].wait()
    place_of = jnp.where(
        lax.broadcasted_iota(jnp.int32, (512, 512), 0) == jnp.broadcast_to(order[...], (512, 512)), 1.0, 0.0
    ).astype(jnp.bfloat16)
    rows_placed = jnp.dot(place_of, matrix[...], preferred_element_type=jnp.float32).astype(jnp.bfloat16)
    mat[...] = lax.dot_general(
        rows_placed, place_of, (((1,), (1,)), ((), ())), preferred_element_type=jnp.float32
    ).astype(jnp.bfloat16)

    sub = lax.broadcasted_iota(jnp.int32, (8, 8, COLS), 1)

    def updated(image, r, h, i, j):
        out = (image - center * ys[r, h, i, j]) * weights[r][0]
        if r > 0:
            out = out - weights[r][1] * ys[r - 1, h, i, j]
        return out

    def store(r, h, i, j, value):
        if r < DEG - 1:
            ys[r + 1, h, i, j] = value
        elif not isinstance(i, int) or i < 7:
            field[h, i, j] = value

    def interior(r, h):
        inner = slice(1, 7)
        for i in range(1, 7):
            value = updated(zs[r, h, i, inner], r, h, i, inner)
            if r == DEG - 1:
                value = jnp.where(sub[1:7] < 7, value, 0.0)
            store(r, h, i, inner, value)

    def border(r, h):
        last = r == DEG - 1
        keep = (lambda v: jnp.where(sub[0, :, :] < 7, v, 0.0)) if last else (lambda v: v)
        for i in range(7 if last else 8):
            edge = i in (0, 7)
            for j in range(8) if edge else (0, 7):
                if last and j == 7:
                    field[h, i, 7] = jnp.zeros((8, COLS), jnp.float32)
                    continue
                image = zs[r, h, i, j]
                a, b = (0 if i == 0 else 1), (0 if j == 0 else 1)
                if edge:
                    image = image + fw[r, h, a, j]
                if j in (0, 7):
                    image = image + fn[r, h, b, i]
                    if edge:
                        image = image + ce[r, h, a, b]
                store(r, h, i, j, keep(updated(image, r, h, i, j)))

    for r in range(DEG):
        for h in range(PART):
            for c in copies[r, h]:
                c.wait_recv()
            if r > 0:
                border(r - 1, h)
            rounded = ys[r, h].reshape(512, COLS).astype(jnp.bfloat16)
            product = jnp.dot(mat[...], rounded, preferred_element_type=jnp.float32).reshape(8, 8, 8, COLS)
            for i in range(8):
                v = product[i]
                joined = jnp.where(
                    sub == 0, pltpu.roll(v, 1, axis=1), jnp.where(sub == 7, pltpu.roll(v, 7, axis=1), 0.0)
                )
                zs[r, h, i] = v + joined
            z, gw, gn, gc = zs.at[r, h], fw.at[r, h], fn.at[r, h], ce.at[r, h]
            both = r < DEG - 1
            cs = [send(z.at[7, 7], gc.at[0, 0], r + 1, h, 2, (wn, nn))]
            if both:
                cs += [
                    send(z.at[0, 0], gc.at[1, 1], r + 1, h, 7, (wp, np_)),
                    send(z.at[7, 0], gc.at[0, 1], r + 1, h, 5, (wn, np_)),
                    send(z.at[0, 7], gc.at[1, 0], r + 1, h, 6, (wp, nn)),
                ]
            cs.append(send(z.at[:, 7], gn.at[0], r + 1, h, 1, (w, nn)))
            if both:
                cs.append(send(z.at[:, 0], gn.at[1], r + 1, h, 4, (w, np_)))
            cs.append(send(z.at[7], gw.at[0], r + 1, h, 0, (wn, n)))
            if both:
                cs.append(send(z.at[0], gw.at[1], r + 1, h, 3, (wp, n)))
            copies[r + 1, h] = cs
            interior(r, h)
    for h in range(PART):
        for c in copies[DEG, h]:
            c.wait_recv()
        border(DEG - 1, h)
        finished(h)
    return pend


def neighbours(w, n):
    return [
        {"wide": (w + a) % WIDE, "narrow": (n + b) % NARROW}
        for a in (WIDE - 1, 0, 1)
        for b in (NARROW - 1, 0, 1)
        if a != 0
    ]


def halves(a):
    high = a.astype(jnp.bfloat16)
    return high, (a - high.astype(jnp.float32)).astype(jnp.bfloat16)


def dot_tn(a, b):
    return lax.dot_general(a, b, (((0,), (0,)), ((), ())), preferred_element_type=jnp.float32)


def gram_tiles(field, tiles):
    cols = []
    per = COLS // 128

    def finished(a):
        cols.append(halves(field[a].reshape(448, COLS)))
        for b in range(a + 1):
            (ah, al), (bh, bl) = cols[a], cols[b]
            block = dot_tn(ah, bh) + (dot_tn(ah, bl) + dot_tn(al, bh))
            for i in range(per):
                for j in range(per):
                    p, q = a * per + i, b * per + j
                    if q <= p:
                        t = 16 * (p * (p + 1) // 2 + q)
                        tiles[t : t + 16] = block[128 * i : 128 * i + 128, 128 * j : 128 * j + 128].reshape(16, 8, 128)

    return finished


def filter_kernel(orbitals, matrix, order, field, full, tiles, held, numbers, lsem, *scratch):
    ys = scratch[1]
    loads = [pltpu.make_async_copy(matrix, held, lsem.at[0])] + [
        pltpu.make_async_copy(
            orbitals.at[:, :, :, COLS * h : COLS * h + COLS], ys.at[0, h, 0:7, 0:7, 0:7], lsem.at[1 + h]
        )
        for h in range(PART)
    ]
    loads.append(pltpu.make_async_copy(order, numbers, lsem.at[1 + PART]))
    for c in loads[1:] + loads[:1]:
        c.start()
    barrier(neighbours(lax.axis_index("wide"), lax.axis_index("narrow")) + peers(*place()))
    pend = filter_steps(gram_tiles(field, tiles), loads, held, numbers, field, *scratch[:8])
    all_reduce(tiles, full, *scratch[8:])
    for c in pend:
        c.wait_send()


def filter_call(orbitals, matrix, order):
    return pl.pallas_call(
        filter_kernel,
        out_shape=(
            jax.ShapeDtypeStruct((PART, 7, 8, 8, COLS), jnp.float32),
            jax.ShapeDtypeStruct((TILES, 8, 128), jnp.float32),
        ),
        in_specs=[pl.BlockSpec(memory_space=pltpu.HBM)] * 3,
        out_specs=[pl.BlockSpec(memory_space=pltpu.VMEM)] * 2,
        scratch_shapes=[
            pltpu.VMEM((TILES, 8, 128), jnp.float32),
            pltpu.VMEM((512, 512), jnp.bfloat16),
            pltpu.VMEM((1, 512), jnp.int32),
            pltpu.SemaphoreType.DMA((2 + PART,)),
        ] + filter_scratch() + ar_scratch(),
        compiler_params=pltpu.CompilerParams(collective_id=0, has_side_effects=True, vmem_limit_bytes=48 << 20),
    )(*(pltpu.with_memory_space_constraint(a, pltpu.HBM) for a in (orbitals, matrix, order)))


def product(a, b, dims):
    (ah, al), (bh, bl) = halves(a), halves(b)

    def one(p, q):
        return lax.dot_general(p, q, (dims, ((), ())), preferred_element_type=jnp.float32)

    return one(ah, bh) + (one(ah, bl) + one(al, bh))


def dot_nt(a, b):
    return product(a, b, ((1,), (1,)))


def reciprocal(d):
    r = pl.reciprocal(d, approx=True)
    return r * (2.0 - d * r)


def thirds(a):
    high = a.astype(jnp.bfloat16).astype(jnp.float32)
    rest = a - high
    middle = rest.astype(jnp.bfloat16).astype(jnp.float32)
    return high, middle, rest - middle


def outer(r, s):
    (rh, rm, rl), (sh, sm, sl) = thirds(r), thirds(s)
    left = jnp.concatenate([rh, rh, rm, rm, rh, rl], axis=0).astype(jnp.bfloat16)
    right = jnp.concatenate([sh, sm, sh, sm, sl, sh], axis=0).astype(jnp.bfloat16)
    return lax.dot_general(left, right, (((0,), (0,)), ((), ())), preferred_element_type=jnp.float32)


def inverse_factor(block):
    rows = [block[8 * i : 8 * i + 8, :] for i in range(16)]
    lane = lax.broadcasted_iota(jnp.int32, (8, 128), 1)
    sub = lax.broadcasted_iota(jnp.int32, (8, 128), 0)
    for b in range(16):
        first = 8 * b
        panel = [jnp.broadcast_to(rows[b][i : i + 1, :], (8, 128)) for i in range(8)]
        e = {}
        for i in range(8):
            for j in range(i, 8):
                e[i, j] = jnp.broadcast_to(panel[i][:, first + j : first + j + 1], (8, 128))
        inside = (lane >= first) & (lane < first + 8)
        p = [jnp.where(inside, jnp.where(lane == first + i, 1.0, 0.0), panel[i]) for i in range(8)]
        if b < 15:
            below = rows[b + 1]
            c = [jnp.broadcast_to(below[:, first + k : first + k + 1], (8, 128)) for k in range(8)]
        inv = [None] * 8
        m = {}
        for k in range(0, 8, 2):
            u, v, t = e[k, k], e[k, k + 1], e[k + 1, k + 1]
            det = u * t - v * v
            over = reciprocal(det)
            iu, iv, it = t * over, v * over, u * over
            inv[k] = reciprocal(u)
            inv[k + 1] = it
            m[k + 1, k] = v * inv[k]
            e[k + 1, k + 1] = det * inv[k]
            for i in range(k + 2, 8):
                f, g = e[k, i], e[k + 1, i]
                one, two = f * iu - g * iv, g * it - f * iv
                for j in range(i, 8):
                    e[i, j] = e[i, j] - (one * e[k, j] + two * e[k + 1, j])
                m[i, k], m[i, k + 1] = f * inv[k], two
            p[k + 1] = p[k + 1] - m[k + 1, k] * p[k]
            for i in range(k + 2, 8):
                p[i] = p[i] - (m[i, k] * p[k] + m[i, k + 1] * p[k + 1])
        own, pivot = p[0], e[0, 0]
        for k in range(1, 8):
            own = jnp.where(sub == k, p[k], own)
            pivot = jnp.where(sub == k, e[k, k], pivot)
        if b < 15:
            s = [p[k] * inv[k] for k in range(8)]
            for l in range(6, -1, -1):
                for k in range(7, l, -1):
                    s[l] = s[l] - m[k, l] * s[k]
            terms = [c[k] * s[k] for k in range(8)]
            while len(terms) > 1:
                terms = [terms[i] + terms[i + 1] for i in range(0, len(terms), 2)]
            fresh = jnp.where(inside, 0.0, below) - terms[0]
            if b < 14:
                change = outer(own, own * reciprocal(pivot))
                for i in range(b + 2, 16):
                    rows[i] = jnp.where(inside, 0.0, rows[i]) - change[8 * i : 8 * i + 8]
            rows[b + 1] = fresh
        y = lax.rsqrt(pivot)
        y = y * (1.5 - 0.5 * pivot * y * y)
        rows[b] = jnp.where(lane <= sub + first, own, 0.0) * y
    return jnp.concatenate(rows, axis=0)


def finish_kernel(node_total, packed, field, out, w, f, held, sems):
    on_diagonal = lax.broadcasted_iota(jnp.int32, (128, 128), 0) == lax.broadcasted_iota(jnp.int32, (128, 128), 1)

    def block(i, j):
        at_tile = 16 * (i * (i + 1) // 2 + j)
        return packed[at_tile : at_tile + 16].reshape(128, 128) * (1.0 / node_total)

    scale_row, scale_column = [], []
    for i in range(4):
        diagonal = jnp.where(on_diagonal, block(i, i), 0.0)
        s = jnp.broadcast_to(lax.rsqrt(jnp.sum(diagonal, axis=0, keepdims=True)), (128, 128))
        scale_row.append(s)
        scale_column.append(jnp.broadcast_to(jnp.sum(jnp.where(on_diagonal, s, 0.0), axis=1, keepdims=True), (128, 128)))
    for i in range(4):
        for j in range(i + 1):
            w[128 * i : 128 * i + 128, 128 * j : 128 * j + 128] = block(i, j) * scale_column[i] * scale_row[j]
    for j in range(4):
        h, q = divmod(128 * j, COLS)
        cols = field[h].reshape(448, COLS)[:, q : q + 128]
        f[:, 128 * j : 128 * j + 128] = cols * scale_row[j][0:1, :]
    stores = []
    for j in range(4):
        here = slice(128 * j, 128 * j + 128)
        inverse = inverse_factor(w[here, here])
        if j < 3:
            column = dot_nt(w[128 * (j + 1) :, here], inverse)
            for i in range(j + 1, 4):
                band = column[128 * (i - j - 1) : 128 * (i - j)]
                w[128 * i : 128 * i + 128, 128 * (j + 1) : 128 * (i + 1)] = w[
                    128 * i : 128 * i + 128, 128 * (j + 1) : 128 * (i + 1)
                ] - dot_nt(band, column[: 128 * (i - j)])
        rotated = dot_nt(f[:, here], inverse)
        held[:, :, :, here] = rotated.reshape(7, 8, 8, 128)
        stores.append(
            pltpu.make_async_copy(held.at[:, 0:7, 0:7, here], out.at[:, :, :, here], sems.at[j])
        )
        stores[j].start()
        if j < 3:
            f[:, 128 * (j + 1) :] = f[:, 128 * (j + 1) :] - dot_nt(rotated, column)
    for c in stores:
        c.wait()


def finish_call(packed, field, node_total):
    return pl.pallas_call(
        functools.partial(finish_kernel, node_total),
        out_shape=jax.ShapeDtypeStruct((7, 7, 7, 512), jnp.float32),
        in_specs=[pl.BlockSpec(memory_space=pltpu.VMEM)] * 2,
        out_specs=pl.BlockSpec(memory_space=pltpu.HBM),
        scratch_shapes=[
            pltpu.VMEM((512, 512), jnp.float32),
            pltpu.VMEM((448, 512), jnp.float32),
            pltpu.VMEM((7, 8, 8, 512), jnp.float32),
            pltpu.SemaphoreType.DMA((4,)),
        ],
        compiler_params=pltpu.CompilerParams(vmem_limit_bytes=40 << 20),
    )(packed, field)


def on_device(orbitals, cell_matrix, cell_order):
    node_total = 343.0 * WIDE * NARROW
    field, total = filter_call(orbitals, cell_matrix.reshape(512, 512), cell_order.reshape(1, 512))
    return finish_call(total, field, node_total)


def solution(mesh):
    return jax.shard_map(
        on_device,
        mesh=mesh,
        in_specs=(
            P("wide", "narrow", None, None),
            P("wide", "narrow", None, None, None),
            P("wide", "narrow", None, None),
        ),
        out_specs=P("wide", "narrow", None, None),
        check_vma=False,
    )
```
